512 devices in a mesh: section: 4 (over x_hi, core), feat: 128 (over y, z, x_lo).
Axes of the slice: x: 4 (x_hi: 2, x_lo: 2; x = x_hi * 2 + x_lo), y: 8, z: 8, core: 2. Of those that a mesh axis runs over, the one named last changes fastest.
Arguments:
- inputs: bfloat16 [4, 128, 8192], P('section', None, 'feat'), may hold values from -6 to 6
- targets: bfloat16 [4, 128, 8192], P('section', None, 'feat'), may hold values from -6 to 6
- enc_w: bfloat16 [4, 4096, 8192], P('section', 'feat'), may hold values from -0.0625 to 0.0625
- enc_b: float32 [4, 4096], P('section', 'feat'), may hold values from -3 to 3
- dec_w: bfloat16 [4, 2, 8192, 4096], P('section', None, 'feat'), may hold values from -0.375 to 0.375
- dec_b: float32 [4, 8192], P('section', 'feat'), may hold values from -3 to 3
Outputs:
- enc_grad: bfloat16 [4, 4096, 8192], P('section', 'feat')
- dec_grad: bfloat16 [4, 2, 8192, 4096], P('section', None, 'feat')
The draws below stay inside these ranges and needn't reach their ends.
All inputs are finite; a program needn't handle non-finite values.
Results may differ from the reference program's by a relative error of at most 0.0058.
Values may be sent and summed in bfloat16 or wider, within the bound.
A program may use at most 64 MiB of HBM per device.

```python
import jax
import jax.numpy as jnp

D = 8192
F = 4096
LAYERS = 4
REACH = 2
TOK = 128


def with_spikes(result, key, source, target, shards_of, factor):
    def block_of(dim):
        return (jnp.arange(result.shape[dim]) // (result.shape[dim] // shards_of)).reshape((-1,) + (1,) * (result.ndim - 1 - dim))

    one_side = jax.random.permutation(key, shards_of)[block_of(target)]
    far = (block_of(target) + shards_of // 2) % shards_of
    return jnp.where((block_of(source) == one_side) | (block_of(source) == far), factor * result, result)


def steps_of(own_key, shape, cuts, low, high):
    def one(axis_at, blocks):
        heights = jax.random.uniform(jax.random.fold_in(jax.random.fold_in(own_key, 6), axis_at), (blocks,), jnp.float32, low / len(cuts), high / len(cuts))
        return jnp.repeat(jnp.exp(heights), shape[axis_at] // blocks).reshape((-1,) + (1,) * (len(shape) - axis_at - 1))

    level = one(*cuts[0])
    for cut in cuts[1:]:
        level = level * one(*cut)
    return level


def bell_draw(stream_key, dims, deviation, most, pieces=(), kind=jnp.bfloat16):
    result = jax.random.normal(stream_key, dims, jnp.float32) * deviation
    if len(pieces) > 0:
        result = steps_of(stream_key, dims, pieces, -0.22, 0.18) * result
    return jnp.clip(result, min=-most, max=most).astype(kind)


def heavy_noise(own_key, dims, spread, most, cuts, heavy, held_as=jnp.bfloat16):
    array = spread * jax.random.normal(own_key, dims, jnp.float32)
    if cuts:
        array = array * steps_of(own_key, dims, cuts, -0.22, 0.18)
    return jnp.clip(with_spikes(array, jax.random.fold_in(own_key, 3), *heavy), -most, most).astype(held_as)


def setup_inputs(seed: int = 0) -> dict:
    streams_of = jax.random.split(jax.random.key(seed), 7)
    return {
        "inputs": bell_draw(streams_of[0], (LAYERS, TOK, D), 1.0, 6.0, ((0, 4), (2, 128))),
        "targets": bell_draw(streams_of[1], (LAYERS, TOK, D), 1.0, 6.0, ((0, 4), (2, 128))),
        "enc_w": bell_draw(streams_of[2], (LAYERS, F, D), D ** -0.5, 0.0625, ((0, 4), (1, 128))),
        "enc_b": bell_draw(streams_of[3], (LAYERS, F), 0.5, 3.0, ((0, 4), (1, 128)), jnp.float32),
        "dec_w": heavy_noise(streams_of[4], (LAYERS, REACH, D, F), F ** -0.5, 0.375, ((0, 4), (2, 128)), (2, 3, 128, 5.5)),
        "dec_b": bell_draw(streams_of[5], (LAYERS, D), 0.5, 3.0, ((0, 4), (1, 128)), jnp.float32),
    }


def reference(inputs, targets, enc_w, enc_b, dec_w, dec_b):
    scale = TOK ** -0.5
    pres = []
    codes = []
    for layer in range(LAYERS):
        pre = jnp.dot(inputs[layer], enc_w[layer].T, preferred_element_type=jnp.float32) + enc_b[layer]
        active = jnp.maximum(pre, 0.0)
        pres.append(active)
        codes.append((active * active).astype(jnp.bfloat16))
    errors = []
    dec_rows = []
    for target_layer in range(LAYERS):
        total = jnp.zeros((TOK, D), jnp.float32) + dec_b[target_layer]
        for offset in range(REACH):
            if offset <= target_layer:
                total = total + jnp.dot(codes[target_layer - offset], dec_w[target_layer, offset].T, preferred_element_type=jnp.float32)
        error = ((total - targets[target_layer].astype(jnp.float32)) * scale).astype(jnp.bfloat16)
        errors.append(error)
        slots = []
        for offset in range(REACH):
            if offset <= target_layer:
                slot = jnp.dot(error.T, codes[target_layer - offset], preferred_element_type=jnp.float32).astype(jnp.bfloat16)
            else:
                slot = jnp.zeros((D, F), jnp.bfloat16)
            slots.append(slot)
        dec_rows.append(jnp.stack(slots))
    enc_rows = []
    for layer in range(LAYERS):
        code_grad = jnp.zeros((TOK, F), jnp.float32)
        for offset in range(REACH):
            if layer + offset < LAYERS:
                code_grad = code_grad + jnp.dot(errors[layer + offset], dec_w[layer + offset, offset], preferred_element_type=jnp.float32)
        pre_grad = (code_grad * 2.0 * pres[layer]).astype(jnp.bfloat16)
        enc_rows.append(jnp.dot(pre_grad.T, inputs[layer], preferred_element_type=jnp.float32).astype(jnp.bfloat16))
    return jnp.stack(enc_rows), jnp.stack(dec_rows)
```

```python
import functools

import jax
import jax.numpy as jnp
from jax import lax
from jax.experimental import pallas as pl
from jax.experimental.pallas import tpu as pltpu
from jax.sharding import PartitionSpec as P

MESH = pl.DeviceIdType.MESH
NY, NZ, NX = 8, 8, 2
BF16, F32 = jnp.bfloat16, jnp.float32


def mod(a, n):
    return lax.rem(a + n, n)


def dot(a, b):
    return jnp.dot(a, b, preferred_element_type=F32)


def dot_nt(a, b):
    return lax.dot_general(a, b, (((1,), (1,)), ((), ())), preferred_element_type=F32)


def column(row):
    n = row.shape[1]
    here = lax.broadcasted_iota(jnp.int32, (n, n), 0) == lax.broadcasted_iota(jnp.int32, (n, n), 1)
    return jnp.sum(jnp.where(here, jnp.broadcast_to(row, (n, n)), 0.0), axis=1, keepdims=True)


def kernel(
    scale, in_ref, tgt_ref, encw_hbm, encb_ref, decw_hbm, decb_ref,
    eg_ref, dg_ref,
    gin, cod, cprev, encw, decw, dwn, wt, err, rprev, rsend, active, part, one_in, two_in, two_out, x_in, x_out,
    load_sem, s_x, r_x, s_one, r_one, s_ring, r_ring, s_sec, r_sec, s_r1, r_r1, s_r2, r_r2,
):
    s = lax.axis_index("section")
    f = lax.axis_index("feat")
    xl = lax.rem(f, NX)
    z = lax.rem(f // NX, NZ)
    y = f // (NX * NZ)

    def at(yy, zz, xx):
        return {"section": s, "feat": (yy * NZ + zz) * NX + xx}

    mate = at(y, z, 1 - xl)
    far_f = (y * NZ + z) * NX + 1 - xl
    odd = lax.rem(s, 2)
    up = {"section": jnp.minimum(s + 1, 3), "feat": jnp.where(odd == 1, far_f, f)}
    down = {"section": jnp.maximum(s - 1, 0), "feat": jnp.where(odd == 0, far_f, f)}
    has_up = s < 3
    has_down = s > 0

    load_e = pltpu.make_async_copy(encw_hbm, encw, load_sem.at[0])
    load_d = pltpu.make_async_copy(decw_hbm, decw, load_sem.at[1])
    load_e.start()
    load_d.start()

    barrier = pltpu.get_barrier_semaphore()
    for j in range(1, NY):
        pl.semaphore_signal(barrier, inc=1, device_id=at(mod(y + j, NY), z, xl), device_id_type=MESH)
    for j in range(1, NZ):
        pl.semaphore_signal(barrier, inc=1, device_id=at(y, mod(z + j, NZ), xl), device_id_type=MESH)
    pl.semaphore_signal(barrier, inc=1, device_id=mate, device_id_type=MESH)

    @pl.when(has_up)
    def _():
        pl.semaphore_signal(barrier, inc=1, device_id=up, device_id_type=MESH)

    @pl.when(has_down)
    def _():
        pl.semaphore_signal(barrier, inc=1, device_id=down, device_id_type=MESH)

    pl.semaphore_wait(barrier, NY + NZ - 1 + jnp.where(has_up, 1, 0) + jnp.where(has_down, 1, 0))

    def remote(src, dst, ss, rs, to):
        return pltpu.make_async_remote_copy(
            src_ref=src, dst_ref=dst, send_sem=ss, recv_sem=rs, device_id=to, device_id_type=MESH
        )

    def slab(buf, c, i, h):
        half = pl.ds(4 * h, 4)
        return buf.at[i, half, 0] if c == 0 else buf.at[half, i, 1]

    def ring_copy(buf, g, c, d, k, h, i):
        step = 1 if d == 0 else -1
        to = at(mod(y + step, NY), z, xl) if c == 0 else at(y, mod(z + step, NZ), xl)
        return remote(slab(buf, c, i, h), slab(buf, c, i, h), s_ring.at[g, c, d, k, h], r_ring.at[g, c, d, k, h], to)

    def gather_start(buf, g):
        own = remote(buf.at[y, z, xl], buf.at[y, z, xl], s_x.at[g], r_x.at[g], mate)
        own.start()

        def line(c):
            copies = []
            for j in range(1, 8):
                to = at(mod(y + j * c, NY), mod(z + j * (1 - c), NZ), xl)
                copies.append(remote(buf.at[y, z, c], buf.at[y, z, c], s_one.at[g, c, j], r_one.at[g, c, j], to))
            for copy in copies:
                copy.start()
            return copies

        first = line(xl)
        own.wait_recv()
        second = line(1 - xl)
        return own, first, second

    def gather_rest(buf, g, own, first, second):
        for copy in first + second:
            copy.wait_recv()
        sent = []
        for c in range(2):
            for h in range(2):
                for d in range(2):
                    copy = ring_copy(buf, g, c, d, 1, h, y if c == 0 else z)
                    copy.start()
                    sent.append(copy)
        for k in range(1, 5):
            for h in range(2):
                for c in range(2):
                    for d in range(2):
                        if k == 4 and h != d:
                            continue
                        step = 1 if d == 0 else -1
                        i = mod((y if c == 0 else z) - step * k, 8)
                        ring_copy(buf, g, c, d, k, h, i).wait_recv()
                        if k < 3 or (k == 3 and h == d):
                            copy = ring_copy(buf, g, c, d, k + 1, h, i)
                            copy.start()
                            sent.append(copy)
        return [own] + first + second + sent

    gin[y, z, xl] = in_ref[...]
    state = gather_start(gin, 0)
    load_e.wait()
    load_d.wait()

    send_w = remote(decw.at[1], dwn, s_sec.at[0], r_sec.at[0], down)

    @pl.when(has_down)
    def _():
        send_w.start()

    sent = gather_rest(gin, 0, *state)

    def pre_step(i, acc):
        return acc + dot(encw[:, pl.ds(pl.multiple_of(i * 1024, 1024), 1024)], gin[i].reshape(1024, 128))

    pre = lax.fori_loop(0, NY, pre_step, jnp.zeros((32, 128), F32)) + column(encb_ref[...])
    act = jnp.maximum(pre, 0.0)
    active[...] = act
    cod[y, z, xl] = (act * act).astype(BF16)
    state = gather_start(cod, 1)

    @pl.when(has_up)
    def _():
        send_w.wait_recv()

    @pl.when(jnp.logical_not(has_up))
    def _():
        dwn[...] = jnp.zeros_like(dwn)
        err[pl.ds(64, 64), :] = jnp.zeros((64, 128), BF16)

    sent += gather_rest(cod, 1, *state)

    def through(weights):
        def step(i, acc):
            return acc + dot(weights[:, pl.ds(pl.multiple_of(i * 512, 512), 512)], cod[i].reshape(512, 128))

        return lax.fori_loop(0, NY, step, jnp.zeros((64, 128), F32))

    send_r = remote(rsend, rprev, s_sec.at[1], r_sec.at[1], up)
    send_c = remote(cod, cprev, s_sec.at[2], r_sec.at[2], up)
    send_e = remote(err.at[pl.ds(0, 64)], err.at[pl.ds(64, 64)], s_sec.at[3], r_sec.at[3], down)

    @pl.when(has_up)
    def _():
        rsend[...] = through(dwn)
        send_r.start()
        send_c.start()

    @pl.when(jnp.logical_not(has_down))
    def _():
        rprev[...] = jnp.zeros_like(rprev)

    total = through(decw.at[0]) + column(decb_ref[...])

    @pl.when(has_down)
    def _():
        send_r.wait_recv()

    total = total + rprev[...]
    err[pl.ds(0, 64), :] = ((total - tgt_ref[...].astype(F32)) * scale).astype(BF16)

    @pl.when(has_down)
    def _():
        send_e.start()

    def decoder_grad(slot, codes):
        def step(i, carry):
            block = dot_nt(err[pl.ds(0, 64), :], codes[i].reshape(512, 128))
            dg_ref[slot, :, pl.ds(pl.multiple_of(i * 512, 512), 512)] = block.astype(BF16)
            return carry

        lax.fori_loop(0, NY, step, 0)

    decoder_grad(0, cod)

    @pl.when(has_up)
    def _():
        send_e.wait_recv()

    def grad_step(i, carry):
        cols = pl.ds(pl.multiple_of(i * 512, 512), 512)
        both = jnp.concatenate([decw[0, :, cols], dwn[:, cols]], axis=0)
        block = lax.dot_general(both, err[...], (((0,), (0,)), ((), ())), preferred_element_type=F32)
        part[i] = block.astype(BF16).reshape(NZ, NX, 32, 128)
        return carry

    lax.fori_loop(0, NY, grad_step, 0)

    ones = []
    for j in range(1, 8):
        yy, zz = mod(y + j, NY), mod(z + j, NZ)
        ones.append(remote(part.at[yy, :, 0], one_in.at[0, j], s_r1.at[0, j], r_r1.at[0, j], at(yy, z, xl)))
        ones.append(remote(part.at[:, zz, 1], one_in.at[1, j], s_r1.at[1, j], r_r1.at[1, j], at(y, zz, xl)))
    for copy in ones:
        copy.start()

    @pl.when(has_down)
    def _():
        send_c.wait_recv()
        decoder_grad(1, cprev)

    @pl.when(jnp.logical_not(has_down))
    def _():
        dg_ref[1] = jnp.zeros((64, 4096), BF16)

    for copy in ones:
        copy.wait_recv()

    def sum_one(c):
        own = part[y, :, 0] if c == 0 else part[:, z, 1]
        acc = own.astype(F32)
        for j in range(1, 8):
            acc = acc + one_in[c, j].astype(F32)
        return acc

    for c in range(2):
        two_out[c] = sum_one(c).astype(BF16)
    twos = []
    for j in range(1, 8):
        yy, zz = mod(y + j, NY), mod(z + j, NZ)
        twos.append(remote(two_out.at[0, zz], two_in.at[0, j], s_r2.at[0, j], r_r2.at[0, j], at(y, zz, xl)))
        twos.append(remote(two_out.at[1, yy], two_in.at[1, j], s_r2.at[1, j], r_r2.at[1, j], at(yy, z, xl)))
    for copy in twos:
        copy.start()
    for copy in twos:
        copy.wait_recv()
    acc0 = two_out[0, z].astype(F32)
    acc1 = two_out[1, y].astype(F32)
    for j in range(1, 8):
        acc0 = acc0 + two_in[0, j].astype(F32)
        acc1 = acc1 + two_in[1, j].astype(F32)
    x_out[...] = jnp.where(xl == 0, acc1, acc0)
    last = remote(x_out, x_in, s_x.at[2], r_x.at[2], mate)
    last.start()
    mine = jnp.where(xl == 0, acc0, acc1)
    last.wait_recv()
    mine = mine + x_in[...]

    pre_grad = (mine * 2.0 * active[...]).astype(BF16)

    def enc_step(i, carry):
        block = dot_nt(pre_grad, gin[i].reshape(1024, 128))
        eg_ref[:, pl.ds(pl.multiple_of(i * 1024, 1024), 1024)] = block.astype(BF16)
        return carry

    lax.fori_loop(0, NY, enc_step, 0)

    for copy in sent + ones + twos + [last]:
        copy.wait_send()

    @pl.when(has_down)
    def _():
        send_w.wait_send()
        send_e.wait_send()

    @pl.when(has_up)
    def _():
        send_r.wait_send()
        send_c.wait_send()


def on_device(inputs, targets, enc_w, enc_b, dec_w, dec_b):
    scale = inputs.shape[1] ** (-0.5)
    vmem = pl.BlockSpec(memory_space=pltpu.VMEM)
    hbm = pl.BlockSpec(memory_space=pl.ANY)
    dma = pltpu.SemaphoreType.DMA
    grid = (NY, NZ, NX, 32, 128)
    eg, dg = pl.pallas_call(
        functools.partial(kernel, scale),
        out_shape=(
            jax.ShapeDtypeStruct((32, 8192), BF16),
            jax.ShapeDtypeStruct((2, 64, 4096), BF16),
        ),
        in_specs=[vmem, vmem, hbm, vmem, hbm, vmem],
        out_specs=(vmem, vmem),
        scratch_shapes=[
            pltpu.VMEM((NY, NZ, NX, 64, 128), BF16),
            pltpu.VMEM(grid, BF16),
            pltpu.VMEM(grid, BF16),
            pltpu.VMEM((32, 8192), BF16),
            pltpu.VMEM((2, 64, 4096), BF16),
            pltpu.VMEM((64, 4096), BF16),
            pltpu.VMEM((8, 128), BF16),
            pltpu.VMEM((128, 128), BF16),
            pltpu.VMEM((64, 128), F32),
            pltpu.VMEM((64, 128), F32),
            pltpu.VMEM((32, 128), F32),
            pltpu.VMEM(grid, BF16),
            pltpu.VMEM((2, 8, 8, 32, 128), BF16),
            pltpu.VMEM((2, 8, 32, 128), BF16),
            pltpu.VMEM((2, 8, 32, 128), BF16),
            pltpu.VMEM((32, 128), F32),
            pltpu.VMEM((32, 128), F32),
            dma((2,)),
            dma((3,)),
            dma((3,)),
            dma((2, 2, 8)),
            dma((2, 2, 8)),
            dma((2, 2, 2, 5, 2)),
            dma((2, 2, 2, 5, 2)),
            dma((4,)),
            dma((4,)),
            dma((2, 8)),
            dma((2, 8)),
            dma((2, 8)),
            dma((2, 8)),
        ],
        compiler_params=pltpu.CompilerParams(collective_id=0, has_side_effects=True),
    )(inputs[0].T, targets[0].T, enc_w[0], enc_b, dec_w[0], dec_b)
    return eg[None], dg[None]


def solution(mesh):
    return jax.shard_map(
        on_device,
        mesh=mesh,
        in_specs=(
            P("section", None, "feat"),
            P("section", None, "feat"),
            P("section", "feat", None),
            P("section", "feat"),
            P("section", None, "feat", None),
            P("section", "feat"),
        ),
        out_specs=(P("section", "feat", None), P("section", None, "feat", None)),
        check_vma=False,
    )
```

```python
import functools

import jax
import jax.numpy as jnp
from jax import lax
from jax.experimental import pallas as pl
from jax.experimental.pallas import tpu as pltpu
from jax.sharding import PartitionSpec as P

MESH = pl.DeviceIdType.MESH
NY, NZ, NX = 8, 8, 2
BF16, F32 = jnp.bfloat16, jnp.float32


def mod(a, n):
    return lax.rem(a + n, n)


def dot(a, b):
    return jnp.dot(a, b, preferred_element_type=F32)


def dot_nt(a, b):
    return lax.dot_general(a, b, (((1,), (1,)), ((), ())), preferred_element_type=F32)


def column(row):
    n = row.shape[1]
    here = lax.broadcasted_iota(jnp.int32, (n, n), 0) == lax.broadcasted_iota(jnp.int32, (n, n), 1)
    return jnp.sum(jnp.where(here, jnp.broadcast_to(row, (n, n)), 0.0), axis=1, keepdims=True)


GROUPS = ((0, 1, -1), (2, -2), (3, -3, 4))
OFFS = tuple(o for group in GROUPS for o in group)


def group_of(o):
    return next(n for n, group in enumerate(GROUPS) if o in group)


def back(o):
    return o if o == 4 else -o


def reach(d, o):
    return 4 if OFFS.index(o) % 2 == d else 3


def travellers(n, d, k):
    return [o for o in GROUPS[n] if k <= reach(d, o)]


PIECES = (4, 4)


def ring_order(g):
    pieces = PIECES[g]
    return [
        (k, h, role, d)
        for k in range(1, 5) for h in range(pieces) for role in range(2) for d in range(2)
        if k < 4 or h // (pieces // 2) == d
    ]


def kernel(
    scale, in_hbm, tgt_hbm, encw_hbm, encb_hbm, decw_hbm, decb_hbm,
    eg_hbm, dg_hbm,
    eg_ref, dg_ref, out_sem, gin, cod, cprev, cown, tgt, encb_ref, decb_ref, encw, decw, dwn, err, rprev, rsend, active, part, ring_in, ring_out, two_in, two_out,
    load_sem, s_line, r_one, s_ring, r_ring, s_sec, r_sec, s_red, r_red, s_two, r_two,
):
    s = lax.axis_index("section")
    f = lax.axis_index("feat")
    xl = lax.rem(f, NX)
    z = lax.rem(f // NX, NZ)
    y = f // (NX * NZ)
    ys = {o: mod(y + o, NY) for o in range(-4, 5)}
    zs = {o: mod(z + o, NZ) for o in range(-4, 5)}

    def at(yy, zz, xx):
        return {"section": s, "feat": (yy * NZ + zz) * NX + xx}

    far_f = (y * NZ + z) * NX + 1 - xl
    odd = lax.rem(s, 2)
    up = {"section": jnp.minimum(s + 1, 3), "feat": jnp.where(odd == 1, far_f, f)}
    down = {"section": jnp.maximum(s - 1, 0), "feat": jnp.where(odd == 0, far_f, f)}
    has_up = s < 3
    has_down = s > 0

    even = xl == 0
    ring = [{o: jnp.where(even, ys[o], zs[o]) for o in ys}, {o: jnp.where(even, zs[o], ys[o]) for o in ys}]
    line = ring[::-1]
    colour = [xl, 1 - xl]

    def along_ring(role, o, xx):
        if role == 0:
            return at(jnp.where(even, ys[o], y), jnp.where(even, z, zs[o]), xx)
        return at(jnp.where(even, y, ys[o]), jnp.where(even, zs[o], z), xx)

    mate = at(y, z, 1 - xl)
    barrier = pltpu.get_barrier_semaphore()
    for o in OFFS:
        if o != 0:
            pl.semaphore_signal(barrier, inc=1, device_id=at(ys[o], z, xl), device_id_type=MESH)
            pl.semaphore_signal(barrier, inc=1, device_id=at(y, zs[o], xl), device_id_type=MESH)
        pl.semaphore_signal(barrier, inc=1, device_id=along_ring(1, o, 1 - xl), device_id_type=MESH)

    @pl.when(has_up)
    def _():
        pl.semaphore_signal(barrier, inc=1, device_id=up, device_id_type=MESH)

    @pl.when(has_down)
    def _():
        pl.semaphore_signal(barrier, inc=1, device_id=down, device_id_type=MESH)

    load_e = pltpu.make_async_copy(encw_hbm, encw, load_sem.at[0])
    load_d = pltpu.make_async_copy(decw_hbm, decw, load_sem.at[1])
    load_t = pltpu.make_async_copy(tgt_hbm, tgt, load_sem.at[2])
    load_b = pltpu.make_async_copy(encb_hbm, encb_ref, load_sem.at[3])
    load_c = pltpu.make_async_copy(decb_hbm, decb_ref, load_sem.at[4])
    for load in (load_d, load_e, load_t, load_b, load_c):
        load.start()

    pl.semaphore_wait(barrier, 22 + jnp.where(has_up, 1, 0) + jnp.where(has_down, 1, 0))

    def remote(src, dst, ss, rs, to):
        return pltpu.make_async_remote_copy(
            src_ref=src, dst_ref=dst, send_sem=ss, recv_sem=rs, device_id=to, device_id_type=MESH
        )

    def arrived(blocks, sem):
        pltpu.make_async_copy(blocks, blocks, sem).wait()

    def place(buf, role, i, o):
        return buf.at[colour[role], ring[role][i], line[role][o]]

    def gather(buf, g, src):
        own = place(buf, 0, 0, 0)
        pltpu.make_async_copy(src, own, r_one.at[g, 0]).start()
        remote(src, own, s_line.at[g], r_one.at[g, 2], mate).start()
        for o in reversed(OFFS):
            if o != 0:
                remote(src, own, s_line.at[g], r_one.at[g, 0], along_ring(1, o, xl)).start()
        other = place(buf, 1, 0, 0)
        arrived(other, r_one.at[g, 2])
        for o in reversed(OFFS):
            if o != 0:
                remote(other, other, s_line.at[g], r_one.at[g, 1], along_ring(0, o, xl)).start()

    def gather_rest(buf, g):
        blocks = 8 // PIECES[g]

        def piece(role, i, h):
            return buf.at[colour[role], ring[role][i], pl.ds(h * blocks, blocks)]

        def send(role, d, k, h):
            ref = piece(role, 1 - k if d == 0 else k - 1, h)
            to = along_ring(role, 1 if d == 0 else -1, xl)
            remote(ref, ref, s_ring.at[g], r_ring.at[g, role, d, k - 1, h], to).start()

        for role in range(2):
            arrived(buf.at[0, 0, pl.ds(0, 8 - role)], r_one.at[g, role])
            for h in range(PIECES[g]):
                for d in range(2):
                    send(role, d, 1, h)
        for k, h, role, d in ring_order(g):
            arrived(piece(role, -k if d == 0 else k, h), r_ring.at[g, role, d, k - 1, h])
            if (k + 1, h, role, d) in ring_order(g):
                send(role, d, k + 1, h)

    def rows_of(buf, i):
        both = jnp.stack([buf[0, i], buf[1, :, i]], axis=1)
        return both.reshape(-1, 128)

    gather(gin, 0, in_hbm)
    load_d.wait()
    send_w = remote(decw.at[1], dwn, s_sec.at[0], r_sec.at[0], down)

    @pl.when(has_down)
    def _():
        send_w.start()

    for load in (load_e, load_t, load_b, load_c):
        load.wait()
    gather_rest(gin, 0)

    def pre_step(i, acc):
        return acc + dot(encw[:, pl.ds(pl.multiple_of(i * 1024, 1024), 1024)], rows_of(gin, i))

    pre = lax.fori_loop(0, NY, pre_step, jnp.zeros((32, 128), F32)) + column(encb_ref[...])
    act = jnp.maximum(pre, 0.0)
    active[...] = act
    cown[...] = (act * act).astype(BF16)
    gather(cod, 1, cown)

    @pl.when(has_up)
    def _():
        send_w.wait_recv()

    @pl.when(jnp.logical_not(has_up))
    def _():
        dwn[...] = jnp.zeros_like(dwn)
        err[pl.ds(64, 64), :] = jnp.zeros((64, 128), BF16)

    gather_rest(cod, 1)

    def through(weights):
        def step(i, acc):
            return acc + dot(weights[:, pl.ds(pl.multiple_of(i * 512, 512), 512)], rows_of(cod, i))

        return lax.fori_loop(0, NY, step, jnp.zeros((64, 128), F32))

    send_r = remote(rsend, rprev, s_sec.at[1], r_sec.at[1], up)
    send_c = remote(cod, cprev, s_sec.at[2], r_sec.at[2], up)
    send_e = remote(err.at[pl.ds(0, 64)], err.at[pl.ds(64, 64)], s_sec.at[3], r_sec.at[3], down)

    @pl.when(has_up)
    def _():
        rsend[...] = through(dwn)
        send_r.start()
        send_c.start()

    @pl.when(jnp.logical_not(has_down))
    def _():
        rprev[...] = jnp.zeros_like(rprev)

    total = through(decw.at[0]) + column(decb_ref[...])

    @pl.when(has_down)
    def _():
        send_r.wait_recv()

    total = total + rprev[...]
    err[pl.ds(0, 64), :] = ((total - tgt[...].astype(F32)) * scale).astype(BF16)

    @pl.when(has_down)
    def _():
        send_e.start()

    def decoder_grad(slot, codes):
        def step(i, carry):
            block = dot_nt(err[pl.ds(0, 64), :], rows_of(codes, i))
            dg_ref[slot, :, pl.ds(pl.multiple_of(i * 512, 512), 512)] = block.astype(BF16)
            return carry

        lax.fori_loop(0, NY, step, 0)

    decoder_grad(0, cod)
    out_0 = pltpu.make_async_copy(dg_ref.at[0], dg_hbm.at[0], out_sem.at[0])
    out_0.start()

    @pl.when(has_up)
    def _():
        send_e.wait_recv()

    def grad_step(i, carry):
        cols = pl.ds(pl.multiple_of(i * 512, 512), 512)
        both = jnp.concatenate([decw[0, :, cols], dwn[:, cols]], axis=0)
        block = lax.dot_general(both, err[...], (((0,), (0,)), ((), ())), preferred_element_type=F32)
        block = block.reshape(NZ, NX, 32, 128)
        part[0, i] = block[:, 0]
        part[1, :, i] = block[:, 1]
        return carry

    lax.fori_loop(0, NY, grad_step, 0)

    def own_part(c, i, o):
        return part[0, ys[i], zs[o]] if c == 0 else part[1, zs[i], ys[o]]

    def ring_to(c, d):
        step = 1 if d == 0 else -1
        return at(ys[step], z, xl) if c == 0 else at(y, zs[step], xl)

    for m in (4, 3, 2, 1):
        for n in reversed(range(len(GROUPS))):
            for c in range(2):
                for d in range(2):
                    passing = travellers(n, d, m + 1)
                    if passing:
                        arrived(ring_in.at[c, d, m, pl.ds(0, len(passing))], r_red.at[c, d, m, n])
                    for o in travellers(n, d, m):
                        slot = OFFS.index(o)
                        value = own_part(c, m if d == 0 else -m, o)
                        if o in passing:
                            value = value + ring_in[c, d, m, slot].astype(F32)
                        ring_out[c, d, m - 1, slot] = value.astype(BF16)
                        remote(
                            ring_out.at[c, d, m - 1, slot], ring_in.at[c, d, m - 1, slot], s_red,
                            r_red.at[c, d, m - 1, n], ring_to(c, d),
                        ).start()

    for n in reversed(range(len(GROUPS))):
        for c in range(2):
            for d in range(2):
                arrived(ring_in.at[c, d, 0, pl.ds(0, len(GROUPS[n]))], r_red.at[c, d, 0, n])
            for o in GROUPS[n]:
                slot = OFFS.index(o)
                value = own_part(c, 0, o)
                for d in range(2):
                    value = value + ring_in[c, d, 0, slot].astype(F32)
                two_out[c, slot] = value.astype(BF16)
                to = at(y, zs[o], 0) if c == 0 else at(ys[o], z, 1)
                send_two = remote(two_out.at[c, slot], two_in.at[xl, OFFS.index(back(o))], s_two, r_two, to)
                if o != 0:
                    send_two.start()
                else:
                    pl.when(xl != c)(send_two.start)

    @pl.when(has_down)
    def _():
        send_c.wait_recv()
        decoder_grad(1, cprev)

    @pl.when(jnp.logical_not(has_down))
    def _():
        dg_ref[1] = jnp.zeros((64, 4096), BF16)

    out_1 = pltpu.make_async_copy(dg_ref.at[1], dg_hbm.at[1], out_sem.at[1])
    out_1.start()
    arrived(cprev.at[0, pl.ds(0, 5), pl.ds(0, 3)], r_two)
    mine = two_out[xl, 0].astype(F32) + two_in[1 - xl, 0].astype(F32)
    for o in OFFS[1:]:
        slot = OFFS.index(o)
        mine = mine + two_in[0, slot].astype(F32) + two_in[1, slot].astype(F32)

    pre_grad = (mine * 2.0 * active[...]).astype(BF16)

    def enc_step(i, carry):
        block = dot_nt(pre_grad, rows_of(gin, i))
        cols = pl.ds(pl.multiple_of(i * 1024, 1024), 1024)
        eg_ref[:, cols] = block.astype(BF16)
        pltpu.make_async_copy(eg_ref.at[:, cols], eg_hbm.at[:, cols], out_sem.at[2]).start()
        return carry

    lax.fori_loop(0, NY, enc_step, 0)

    pltpu.make_async_copy(eg_ref, eg_hbm, out_sem.at[2]).wait()
    out_0.wait()
    out_1.wait()
    for g, buf in enumerate((gin, cod)):
        arrived(buf.at[0, pl.ds(0, 5), pl.ds(0, 3)], s_line.at[g])
        arrived(buf.at[:, pl.ds(0, 7)], s_ring.at[g])
    arrived(ring_out.at[:, :, :, pl.ds(0, 7)], s_red)
    arrived(cprev.at[0, pl.ds(0, 5), pl.ds(0, 3)], s_two)

    @pl.when(has_down)
    def _():
        send_w.wait_send()
        send_e.wait_send()

    @pl.when(has_up)
    def _():
        send_r.wait_send()
        send_c.wait_send()


def on_device(inputs, targets, enc_w, enc_b, dec_w, dec_b):
    scale = inputs.shape[1] ** (-0.5)
    vmem = pl.BlockSpec(memory_space=pltpu.VMEM)
    hbm = pl.BlockSpec(memory_space=pltpu.HBM)
    dma = pltpu.SemaphoreType.DMA
    grid = (NX, 8, 8, 32, 128)
    eg, dg = pl.pallas_call(
        functools.partial(kernel, scale),
        out_shape=(
            jax.ShapeDtypeStruct((32, 8192), BF16),
            jax.ShapeDtypeStruct((2, 64, 4096), BF16),
        ),
        in_specs=[hbm] * 6,
        out_specs=(hbm, hbm),
        scratch_shapes=[
            pltpu.VMEM((32, 8192), BF16),
            pltpu.VMEM((2, 64, 4096), BF16),
            dma((3,)),
            pltpu.VMEM((NX, 8, 8, 64, 128), BF16),
            pltpu.VMEM(grid, BF16),
            pltpu.VMEM(grid, BF16),
            pltpu.VMEM((32, 128), BF16),
            pltpu.VMEM((64, 128), BF16),
            pltpu.VMEM((1, 32), F32),
            pltpu.VMEM((1, 64), F32),
            pltpu.VMEM((32, 8192), BF16),
            pltpu.VMEM((2, 64, 4096), BF16),
            pltpu.VMEM((64, 4096), BF16),
            pltpu.VMEM((128, 128), BF16),
            pltpu.VMEM((64, 128), F32),
            pltpu.VMEM((64, 128), F32),
            pltpu.VMEM((32, 128), F32),
            pltpu.VMEM(grid, F32),
            pltpu.VMEM((2, 2, 4, 8, 32, 128), BF16),
            pltpu.VMEM((2, 2, 4, 8, 32, 128), BF16),
            pltpu.VMEM((2, 8, 32, 128), BF16),
            pltpu.VMEM((2, 8, 32, 128), BF16),
            dma((5,)),
            dma((2,)),
            dma((2, 3)),
            dma((2,)),
            dma((2, 2, 2, 4, max(PIECES))),
            dma((4,)),
            dma((4,)),
            dma,
            dma((2, 2, 4, 3)),
            dma,
            dma,
        ],
        compiler_params=pltpu.CompilerParams(collective_id=0, has_side_effects=True),
    )(inputs[0].T, targets[0].T, enc_w[0], enc_b, dec_w[0], dec_b)
    return eg[None], dg[None]


def solution(mesh):
    return jax.shard_map(
        on_device,
        mesh=mesh,
        in_specs=(
            P("section", None, "feat"),
            P("section", None, "feat"),
            P("section", "feat", None),
            P("section", "feat"),
            P("section", None, "feat", None),
            P("section", "feat"),
        ),
        out_specs=(P("section", "feat", None), P("section", None, "feat", None)),
        check_vma=False,
    )
```

```python
import functools

import jax
import jax.numpy as jnp
from jax import lax
from jax.experimental import pallas as pl
from jax.experimental.pallas import tpu as pltpu
from jax.sharding import PartitionSpec as P

MESH = pl.DeviceIdType.MESH
NY, NZ, NX = 8, 8, 2
BF16, F32 = jnp.bfloat16, jnp.float32


def mod(a, n):
    return lax.rem(a + n, n)


def dot(a, b):
    return jnp.dot(a, b, preferred_element_type=F32)


def dot_nt(a, b):
    return lax.dot_general(a, b, (((1,), (1,)), ((), ())), preferred_element_type=F32)


def column(row):
    n = row.shape[1]
    here = lax.broadcasted_iota(jnp.int32, (n, n), 0) == lax.broadcasted_iota(jnp.int32, (n, n), 1)
    return jnp.sum(jnp.where(here, jnp.broadcast_to(row, (n, n)), 0.0), axis=1, keepdims=True)


GROUPS = ((0, 1, -1), (2, -2), (3, -3, 4))
OFFS = tuple(o for group in GROUPS for o in group)


def group_of(o):
    return next(n for n, group in enumerate(GROUPS) if o in group)


def back(o):
    return o if o == 4 else -o


def reach(d, o):
    return 4 if OFFS.index(o) % 2 == d else 3


def travellers(n, d, k):
    return [o for o in GROUPS[n] if k <= reach(d, o)]


PIECES = (2, 2)
LEVELS = (2, 1, 3, 4)


def carries(g, k, h, d):
    return k < 4 or (d == 0 if PIECES[g] == 1 else h // (PIECES[g] // 2) == d)


def kernel(
    scale, in_hbm, tgt_hbm, encw_hbm, encb_hbm, decw_hbm, decb_hbm,
    eg_hbm, dg_hbm,
    eg_ref, dg_ref, out_sem, gin, cod, cprev, cown, tgt, encb_ref, decb_ref, encw, decw, dwn, err, rprev, sums, encp, wt, wp, active, part, ring_in, ring_out, two_in, two_out,
    load_sem, s_line, r_one, s_ring, r_ring, s_sec, r_sec, s_red, r_red, s_two, r_two,
):
    s = lax.axis_index("section")
    f = lax.axis_index("feat")
    xl = lax.rem(f, NX)
    z = lax.rem(f // NX, NZ)
    y = f // (NX * NZ)
    ys = {o: mod(y + o, NY) for o in range(-4, 5)}
    zs = {o: mod(z + o, NZ) for o in range(-4, 5)}

    def at(yy, zz, xx):
        return {"section": s, "feat": (yy * NZ + zz) * NX + xx}

    far_f = (y * NZ + z) * NX + 1 - xl
    odd = lax.rem(s, 2)
    up = {"section": jnp.minimum(s + 1, 3), "feat": jnp.where(odd == 1, far_f, f)}
    down = {"section": jnp.maximum(s - 1, 0), "feat": jnp.where(odd == 0, far_f, f)}
    has_up = s < 3
    has_down = s > 0

    even = xl == 0
    ring = [{o: jnp.where(even, ys[o], zs[o]) for o in ys}, {o: jnp.where(even, zs[o], ys[o]) for o in ys}]
    line = ring[::-1]
    colour = [xl, 1 - xl]

    def along_ring(role, o, xx):
        if role == 0:
            return at(jnp.where(even, ys[o], y), jnp.where(even, z, zs[o]), xx)
        return at(jnp.where(even, y, ys[o]), jnp.where(even, zs[o], z), xx)

    mate = at(y, z, 1 - xl)
    barrier = pltpu.get_barrier_semaphore()
    for o in OFFS:
        if o != 0:
            pl.semaphore_signal(barrier, inc=1, device_id=at(ys[o], z, xl), device_id_type=MESH)
            pl.semaphore_signal(barrier, inc=1, device_id=at(y, zs[o], xl), device_id_type=MESH)
        pl.semaphore_signal(barrier, inc=1, device_id=along_ring(1, o, 1 - xl), device_id_type=MESH)

    @pl.when(has_up)
    def _():
        pl.semaphore_signal(barrier, inc=1, device_id=up, device_id_type=MESH)

    @pl.when(has_down)
    def _():
        pl.semaphore_signal(barrier, inc=1, device_id=down, device_id_type=MESH)

    load_e = pltpu.make_async_copy(encw_hbm, encw, load_sem.at[0])
    load_d = pltpu.make_async_copy(decw_hbm, decw, load_sem.at[1])
    load_t = pltpu.make_async_copy(tgt_hbm, tgt, load_sem.at[2])
    load_b = pltpu.make_async_copy(encb_hbm, encb_ref, load_sem.at[3])
    load_c = pltpu.make_async_copy(decb_hbm, decb_ref, load_sem.at[4])
    for load in (load_d, load_e, load_t, load_b, load_c):
        load.start()

    pl.semaphore_wait(barrier, 22 + jnp.where(has_up, 1, 0) + jnp.where(has_down, 1, 0))

    def remote(src, dst, ss, rs, to):
        return pltpu.make_async_remote_copy(
            src_ref=src, dst_ref=dst, send_sem=ss, recv_sem=rs, device_id=to, device_id_type=MESH
        )

    def arrived(blocks, sem):
        pltpu.make_async_copy(blocks, blocks, sem).wait()

    def place(buf, role, i, o):
        return buf.at[colour[role], ring[role][i], line[role][o]]

    def gather(buf, g, src, meanwhile):
        own = place(buf, 0, 0, 0)
        pltpu.make_async_copy(src, own, r_one.at[g, 0]).start()
        remote(src, own, s_line.at[g], r_one.at[g, 2], mate).start()
        for o in reversed(OFFS):
            if o != 0:
                remote(src, own, s_line.at[g], r_one.at[g, 0], along_ring(1, o, xl)).start()
        meanwhile(-2)
        other = place(buf, 1, 0, 0)
        arrived(other, r_one.at[g, 2])
        for o in reversed(OFFS):
            if o != 0:
                remote(other, other, s_line.at[g], r_one.at[g, 1], along_ring(0, o, xl)).start()

    def gather_rest(buf, g, meanwhile):
        meanwhile(-1)
        blocks = 8 // PIECES[g]

        def piece(role, i, h):
            return buf.at[colour[role], ring[role][i], pl.ds(h * blocks, blocks)]

        def send(role, d, k, h):
            way = 1 if d == 0 else -1
            ref = piece(role, 0 if k < 3 else -2 * way, h)
            to = along_ring(role, way if k in (1, 3) else 2 * way, xl)
            remote(ref, ref, s_ring.at[g], r_ring.at[g, role, d, k - 1, h], to).start()

        for role in range(2):
            arrived(buf.at[0, 0, pl.ds(0, 8 - role)], r_one.at[g, role])
            for k in (2, 1):
                for h in range(PIECES[g]):
                    for d in range(2):
                        send(role, d, k, h)
        meanwhile(0)
        for k in LEVELS:
            for h in range(PIECES[g]):
                for role in range(2):
                    for d in range(2):
                        if carries(g, k, h, d):
                            arrived(piece(role, -k if d == 0 else k, h), r_ring.at[g, role, d, k - 1, h])
                        if k == 2:
                            for further in (4, 3):
                                if carries(g, further, h, d):
                                    send(role, d, further, h)
            meanwhile(k)

    def rows_of(buf, i):
        both = jnp.stack([buf[0, i], buf[1, :, i]], axis=1)
        return both.reshape(-1, 128)

    send_w = remote(decw.at[1], dwn, s_sec.at[0], r_sec.at[0], down)

    def at_distance(k):
        return (k,) if k in (0, 4) else (k, -k)

    def sort_encoder(i, carry):
        for j in range(4):
            for c in range(2):
                halves = []
                for o in (2 * j, 2 * j + 1):
                    base = i * 1024 + o * 128 if c == 0 else o * 1024 + i * 128
                    group = encw[:, pl.ds(pl.multiple_of(base, 128), 128)]
                    halves.append(group[:, c * 64 : c * 64 + 64])
                encp[c, i, :, j * 128 : j * 128 + 128] = jnp.concatenate(halves, axis=1)
        return carry

    def turn_decoders(i, carry):
        for q in range(4):
            cols = pl.ds(pl.multiple_of(i * 512 + q * 128, 128), 128)
            tile = jnp.concatenate([decw[0, :, cols], dwn[:, cols]], axis=0).T
            for o in range(2):
                wt[0, i, 2 * q + o] = tile[o * 64 : o * 64 + 32]
                wt[1, 2 * q + o, i] = tile[o * 64 + 32 : o * 64 + 64]
        return carry

    def during_inputs(k):
        if k == -2:
            load_d.wait()
            pl.when(has_down)(send_w.start)
            sums[...] = jnp.zeros_like(sums)
            active[...] = jnp.zeros_like(active)
        elif k == -1:
            for load in (load_e, load_t, load_b, load_c):
                load.wait()
            lax.fori_loop(0, 8, sort_encoder, 0)
        else:
            acc = active[...]
            for i in at_distance(k):
                for role in range(2):
                    c, r = colour[role], ring[role][i]
                    acc = acc + dot(encp[c, r], gin[c, r].reshape(512, 128))
            active[...] = acc
        if k == LEVELS[0]:
            pl.when(has_up)(send_w.wait_recv)

            @pl.when(jnp.logical_not(has_up))
            def _():
                dwn[...] = jnp.zeros_like(dwn)
                err[pl.ds(64, 64), :] = jnp.zeros((64, 128), BF16)

        if k in LEVELS[:3]:
            turn = 3 * LEVELS.index(k)
            lax.fori_loop(turn, min(turn + 3, 8), turn_decoders, 0)

    def sort_decoders(i, carry):
        for c in range(2):
            wp[c, i] = wt[c, i].reshape(256, 128).T
        return carry

    def during_codes(k):
        if k == -1:
            lax.fori_loop(0, 8, sort_decoders, 0)
        elif k >= 0:
            acc = sums[...]
            for i in at_distance(k):
                for role in range(2):
                    c, r = colour[role], ring[role][i]
                    acc = acc + dot(wp[c, r], cod[c, r].reshape(256, 128))
            sums[...] = acc

    gather(gin, 0, in_hbm, during_inputs)
    gather_rest(gin, 0, during_inputs)

    pre = active[...] + column(encb_ref[...])
    act = jnp.maximum(pre, 0.0)
    active[...] = act
    cown[...] = (act * act).astype(BF16)
    gather(cod, 1, cown, during_codes)
    gather_rest(cod, 1, during_codes)

    send_r = remote(sums.at[pl.ds(64, 64)], rprev, s_sec.at[1], r_sec.at[1], up)
    send_c = remote(cod, cprev, s_sec.at[2], r_sec.at[2], up)
    send_e = remote(err.at[pl.ds(0, 64)], err.at[pl.ds(64, 64)], s_sec.at[3], r_sec.at[3], down)

    @pl.when(has_up)
    def _():
        send_r.start()
        send_c.start()

    @pl.when(jnp.logical_not(has_down))
    def _():
        rprev[...] = jnp.zeros_like(rprev)

    total = sums[pl.ds(0, 64), :] + column(decb_ref[...])

    @pl.when(has_down)
    def _():
        send_r.wait_recv()

    total = total + rprev[...]
    err[pl.ds(0, 64), :] = ((total - tgt[...].astype(F32)) * scale).astype(BF16)

    @pl.when(has_down)
    def _():
        send_e.start()

    def decoder_grad(slot, codes):
        def step(i, carry):
            block = dot_nt(err[pl.ds(0, 64), :], rows_of(codes, i))
            dg_ref[slot, :, pl.ds(pl.multiple_of(i * 512, 512), 512)] = block.astype(BF16)
            return carry

        lax.fori_loop(0, NY, step, 0)

    decoder_grad(0, cod)
    out_0 = pltpu.make_async_copy(dg_ref.at[0], dg_hbm.at[0], out_sem.at[0])
    out_0.start()

    @pl.when(has_up)
    def _():
        send_e.wait_recv()

    def own_part(c, i, o):
        return part[0, ys[i], zs[o]] if c == 0 else part[1, zs[i], ys[o]]

    def ring_to(c, d):
        step = 1 if d == 0 else -1
        return at(ys[step], z, xl) if c == 0 else at(y, zs[step], xl)

    def grad_slabs(m):
        for i in at_distance(m):
            for c, r in ((0, ys[i]), (1, zs[i])):
                part[c, r] = dot(wt[c, r].reshape(256, 128), err[...]).reshape(8, 32, 128)

    for m in (4, 3, 2, 1):
        grad_slabs(m)
        for n in reversed(range(len(GROUPS))):
            for c in range(2):
                for d in range(2):
                    passing = travellers(n, d, m + 1)
                    if passing:
                        arrived(ring_in.at[c, d, m, pl.ds(0, len(passing))], r_red.at[c, d, m, n])
                    for o in travellers(n, d, m):
                        slot = OFFS.index(o)
                        value = own_part(c, m if d == 0 else -m, o)
                        if o in passing:
                            value = value + ring_in[c, d, m, slot].astype(F32)
                        ring_out[c, d, m - 1, slot] = value.astype(BF16)
                        remote(
                            ring_out.at[c, d, m - 1, slot], ring_in.at[c, d, m - 1, slot], s_red,
                            r_red.at[c, d, m - 1, n], ring_to(c, d),
                        ).start()

    grad_slabs(0)
    for n in reversed(range(len(GROUPS))):
        for c in range(2):
            for d in range(2):
                arrived(ring_in.at[c, d, 0, pl.ds(0, len(GROUPS[n]))], r_red.at[c, d, 0, n])
            for o in GROUPS[n]:
                slot = OFFS.index(o)
                value = own_part(c, 0, o)
                for d in range(2):
                    value = value + ring_in[c, d, 0, slot].astype(F32)
                two_out[c, slot] = value.astype(BF16)
                to = at(y, zs[o], 0) if c == 0 else at(ys[o], z, 1)
                send_two = remote(two_out.at[c, slot], two_in.at[xl, OFFS.index(back(o))], s_two, r_two, to)
                if o != 0:
                    send_two.start()
                else:
                    pl.when(xl != c)(send_two.start)

    @pl.when(has_down)
    def _():
        send_c.wait_recv()
        decoder_grad(1, cprev)

    @pl.when(jnp.logical_not(has_down))
    def _():
        dg_ref[1] = jnp.zeros((64, 4096), BF16)

    out_1 = pltpu.make_async_copy(dg_ref.at[1], dg_hbm.at[1], out_sem.at[1])
    out_1.start()
    arrived(cprev.at[0, pl.ds(0, 5), pl.ds(0, 3)], r_two)
    mine = two_out[xl, 0].astype(F32) + two_in[1 - xl, 0].astype(F32)
    for o in OFFS[1:]:
        slot = OFFS.index(o)
        mine = mine + two_in[0, slot].astype(F32) + two_in[1, slot].astype(F32)

    pre_grad = (mine * 2.0 * active[...]).astype(BF16)

    def enc_step(i, carry):
        block = dot_nt(pre_grad, rows_of(gin, i))
        cols = pl.ds(pl.multiple_of(i * 1024, 1024), 1024)
        eg_ref[:, cols] = block.astype(BF16)
        pltpu.make_async_copy(eg_ref.at[:, cols], eg_hbm.at[:, cols], out_sem.at[2]).start()
        return carry

    lax.fori_loop(0, NY, enc_step, 0)

    pltpu.make_async_copy(eg_ref, eg_hbm, out_sem.at[2]).wait()
    out_0.wait()
    out_1.wait()
    for g, buf in enumerate((gin, cod)):
        arrived(buf.at[0, pl.ds(0, 5), pl.ds(0, 3)], s_line.at[g])
        arrived(buf.at[:, pl.ds(0, 7)], s_ring.at[g])
    arrived(ring_out.at[:, :, :, pl.ds(0, 7)], s_red)
    arrived(cprev.at[0, pl.ds(0, 5), pl.ds(0, 3)], s_two)

    @pl.when(has_down)
    def _():
        send_w.wait_send()
        send_e.wait_send()

    @pl.when(has_up)
    def _():
        send_r.wait_send()
        send_c.wait_send()


def on_device(inputs, targets, enc_w, enc_b, dec_w, dec_b):
    scale = inputs.shape[1] ** (-0.5)
    vmem = pl.BlockSpec(memory_space=pltpu.VMEM)
    hbm = pl.BlockSpec(memory_space=pltpu.HBM)
    dma = pltpu.SemaphoreType.DMA
    grid = (NX, 8, 8, 32, 128)
    eg, dg = pl.pallas_call(
        functools.partial(kernel, scale),
        out_shape=(
            jax.ShapeDtypeStruct((32, 8192), BF16),
            jax.ShapeDtypeStruct((2, 64, 4096), BF16),
        ),
        in_specs=[hbm] * 6,
        out_specs=(hbm, hbm),
        scratch_shapes=[
            pltpu.VMEM((32, 8192), BF16),
            pltpu.VMEM((2, 64, 4096), BF16),
            dma((3,)),
            pltpu.VMEM((NX, 8, 8, 64, 128), BF16),
            pltpu.VMEM(grid, BF16),
            pltpu.VMEM(grid, BF16),
            pltpu.VMEM((32, 128), BF16),
            pltpu.VMEM((64, 128), BF16),
            pltpu.VMEM((1, 32), F32),
            pltpu.VMEM((1, 64), F32),
            pltpu.VMEM((32, 8192), BF16),
            pltpu.VMEM((2, 64, 4096), BF16),
            pltpu.VMEM((64, 4096), BF16),
            pltpu.VMEM((128, 128), BF16),
            pltpu.VMEM((64, 128), F32),
            pltpu.VMEM((128, 128), F32),
            pltpu.VMEM((NX, 8, 32, 512), BF16),
            pltpu.VMEM(grid, BF16),
            pltpu.VMEM((NX, 8, 128, 256), BF16),
            pltpu.VMEM((32, 128), F32),
            pltpu.VMEM(grid, F32),
            pltpu.VMEM((2, 2, 4, 8, 32, 128), BF16),
            pltpu.VMEM((2, 2, 4, 8, 32, 128), BF16),
            pltpu.VMEM((2, 8, 32, 128), BF16),
            pltpu.VMEM((2, 8, 32, 128), BF16),
            dma((5,)),
            dma((2,)),
            dma((2, 3)),
            dma((2,)),
            dma((2, 2, 2, 4, max(PIECES))),
            dma((4,)),
            dma((4,)),
            dma,
            dma((2, 2, 4, 3)),
            dma,
            dma,
        ],
        compiler_params=pltpu.CompilerParams(collective_id=0, has_side_effects=True),
    )(inputs[0].T, targets[0].T, enc_w[0], enc_b, dec_w[0], dec_b)
    return eg[None], dg[None]


def solution(mesh):
    return jax.shard_map(
        on_device,
        mesh=mesh,
        in_specs=(
            P("section", None, "feat"),
            P("section", None, "feat"),
            P("section", "feat", None),
            P("section", "feat"),
            P("section", None, "feat", None),
            P("section", "feat"),
        ),
        out_specs=(P("section", "feat", None), P("section", None, "feat", None)),
        check_vma=False,
    )
```

```python
import functools

import jax
import jax.numpy as jnp
from jax import lax
from jax.experimental import pallas as pl
from jax.experimental.pallas import tpu as pltpu
from jax.sharding import PartitionSpec as P

MESH = pl.DeviceIdType.MESH
NY, NZ, NX = 8, 8, 2
BF16, F32 = jnp.bfloat16, jnp.float32


def mod(a, n):
    return lax.rem(a + n, n)


def dot(a, b):
    return jnp.dot(a, b, preferred_element_type=F32)


def dot_nt(a, b):
    return lax.dot_general(a, b, (((1,), (1,)), ((), ())), preferred_element_type=F32)


def column(row):
    n = row.shape[1]
    here = lax.broadcasted_iota(jnp.int32, (n, n), 0) == lax.broadcasted_iota(jnp.int32, (n, n), 1)
    return jnp.sum(jnp.where(here, jnp.broadcast_to(row, (n, n)), 0.0), axis=1, keepdims=True)


GROUPS = ((0, 1, -1), (2, -2), (3, -3, 4))
OFFS = tuple(o for group in GROUPS for o in group)


def group_of(o):
    return next(n for n, group in enumerate(GROUPS) if o in group)


def back(o):
    return o if o == 4 else -o


def reach(d, o):
    return 4 if OFFS.index(o) % 2 == d else 3


def travellers(n, d, k):
    return [o for o in GROUPS[n] if k <= reach(d, o)]


PIECES = (4, 2)
LEVELS = ((1, 2, 3, 4), (2, 1, 3, 4))
CROSS = (True, True)


def carries(g, k, h, d):
    return k < 4 or (d == 0 if PIECES[g] == 1 else h // (PIECES[g] // 2) == d)


def kernel(
    scale, in_hbm, tgt_hbm, encw_hbm, encb_hbm, decw_hbm, decb_hbm,
    eg_hbm, dg_hbm,
    eg_ref, dg_ref, out_sem, gin, cod, cprev, cown, tgt, encb_ref, decb_ref, encw, decw, dwn, err, rprev, sums, encp, wt, wp, active, part, ring_in, ring_out, two_in, two_out,
    load_sem, s_line, r_one, s_ring, r_ring, s_sec, r_sec, s_red, r_red, s_two, r_two,
):
    s = lax.axis_index("section")
    f = lax.axis_index("feat")
    xl = lax.rem(f, NX)
    z = lax.rem(f // NX, NZ)
    y = f // (NX * NZ)
    ys = {o: mod(y + o, NY) for o in range(-4, 5)}
    zs = {o: mod(z + o, NZ) for o in range(-4, 5)}

    def at(yy, zz, xx):
        return {"section": s, "feat": (yy * NZ + zz) * NX + xx}

    far_f = (y * NZ + z) * NX + 1 - xl
    odd = lax.rem(s, 2)
    up = {"section": jnp.minimum(s + 1, 3), "feat": jnp.where(odd == 1, far_f, f)}
    down = {"section": jnp.maximum(s - 1, 0), "feat": jnp.where(odd == 0, far_f, f)}
    has_up = s < 3
    has_down = s > 0

    even = xl == 0
    ring = [{o: jnp.where(even, ys[o], zs[o]) for o in ys}, {o: jnp.where(even, zs[o], ys[o]) for o in ys}]
    line = ring[::-1]
    colour = [xl, 1 - xl]

    def along_ring(role, o, xx):
        if role == 0:
            return at(jnp.where(even, ys[o], y), jnp.where(even, z, zs[o]), xx)
        return at(jnp.where(even, y, ys[o]), jnp.where(even, zs[o], z), xx)

    mate = at(y, z, 1 - xl)
    barrier = pltpu.get_barrier_semaphore()
    for o in OFFS:
        if o != 0:
            pl.semaphore_signal(barrier, inc=1, device_id=at(ys[o], z, xl), device_id_type=MESH)
            pl.semaphore_signal(barrier, inc=1, device_id=at(y, zs[o], xl), device_id_type=MESH)
        pl.semaphore_signal(barrier, inc=1, device_id=along_ring(1, o, 1 - xl), device_id_type=MESH)
        if o != 0:
            pl.semaphore_signal(barrier, inc=1, device_id=along_ring(0, o, 1 - xl), device_id_type=MESH)

    @pl.when(has_up)
    def _():
        pl.semaphore_signal(barrier, inc=1, device_id=up, device_id_type=MESH)

    @pl.when(has_down)
    def _():
        pl.semaphore_signal(barrier, inc=1, device_id=down, device_id_type=MESH)

    load_e = pltpu.make_async_copy(encw_hbm, encw, load_sem.at[0])
    load_d = pltpu.make_async_copy(decw_hbm, decw, load_sem.at[1])
    load_t = pltpu.make_async_copy(tgt_hbm, tgt, load_sem.at[2])
    load_b = pltpu.make_async_copy(encb_hbm, encb_ref, load_sem.at[3])
    load_c = pltpu.make_async_copy(decb_hbm, decb_ref, load_sem.at[4])
    for load in (load_d, load_e, load_t, load_b, load_c):
        load.start()

    pl.semaphore_wait(barrier, 29 + jnp.where(has_up, 1, 0) + jnp.where(has_down, 1, 0))

    def remote(src, dst, ss, rs, to):
        return pltpu.make_async_remote_copy(
            src_ref=src, dst_ref=dst, send_sem=ss, recv_sem=rs, device_id=to, device_id_type=MESH
        )

    def arrived(blocks, sem):
        pltpu.make_async_copy(blocks, blocks, sem).wait()

    def place(buf, role, i, o):
        return buf.at[colour[role], ring[role][i], line[role][o]]

    def gather(buf, g, src, meanwhile):
        own = place(buf, 0, 0, 0)
        pltpu.make_async_copy(src, own, r_one.at[g, 0]).start()
        if CROSS[g]:
            for o in reversed(OFFS):
                remote(src, own, s_line.at[g], r_one.at[g, 1], along_ring(1, o, 1 - xl)).start()
                if o != 0:
                    remote(src, own, s_line.at[g], r_one.at[g, 0], along_ring(1, o, xl)).start()
            meanwhile(-2)
            return
        remote(src, own, s_line.at[g], r_one.at[g, 2], mate).start()
        for o in reversed(OFFS):
            if o != 0:
                remote(src, own, s_line.at[g], r_one.at[g, 0], along_ring(1, o, xl)).start()
        meanwhile(-2)
        other = place(buf, 1, 0, 0)
        arrived(other, r_one.at[g, 2])
        for o in reversed(OFFS):
            if o != 0:
                remote(other, other, s_line.at[g], r_one.at[g, 1], along_ring(0, o, xl)).start()

    def gather_rest(buf, g, meanwhile):
        meanwhile(-1)
        blocks = 8 // PIECES[g]

        def piece(role, i, h):
            return buf.at[colour[role], ring[role][i], pl.ds(h * blocks, blocks)]

        def send(role, d, k, h):
            way = 1 if d == 0 else -1
            chain = LEVELS[g][0] == 1
            ref = piece(role, -2 * way if k > 2 else -way if k == 2 and chain else 0, h)
            to = along_ring(role, way if k in (1, 3) or k == 2 and chain else 2 * way, xl)
            remote(ref, ref, s_ring.at[g], r_ring.at[g, role, d, k - 1, h], to).start()

        for role in range(2):
            arrived(buf.at[0, 0, pl.ds(0, 8 if CROSS[g] else 8 - role)], r_one.at[g, role])
            for k in (2, 1) if LEVELS[g][0] == 2 else (1,):
                for h in range(PIECES[g]):
                    for d in range(2):
                        send(role, d, k, h)
        meanwhile(0)
        for k in LEVELS[g]:
            for h in range(PIECES[g]):
                for role in range(2):
                    for d in range(2):
                        if carries(g, k, h, d):
                            arrived(piece(role, -k if d == 0 else k, h), r_ring.at[g, role, d, k - 1, h])
                        if k == 1 and LEVELS[g][0] == 1:
                            send(role, d, 2, h)
                        if k == 2:
                            for further in (4, 3):
                                if carries(g, further, h, d):
                                    send(role, d, further, h)
            meanwhile(k)

    def rows_of(buf, i):
        both = jnp.stack([buf[0, i], buf[1, :, i]], axis=1)
        return both.reshape(-1, 128)

    send_w = remote(decw.at[1], dwn, s_sec.at[0], r_sec.at[0], down)

    def at_distance(k):
        return (k,) if k in (0, 4) else (k, -k)

    def sort_encoder(i, carry):
        for j in range(4):
            for c in range(2):
                halves = []
                for o in (2 * j, 2 * j + 1):
                    base = i * 1024 + o * 128 if c == 0 else o * 1024 + i * 128
                    group = encw[:, pl.ds(pl.multiple_of(base, 128), 128)]
                    halves.append(group[:, c * 64 : c * 64 + 64])
                encp[c, i, :, j * 128 : j * 128 + 128] = jnp.concatenate(halves, axis=1)
        return carry

    def turn_decoders(i, carry):
        for q in range(4):
            cols = pl.ds(pl.multiple_of(i * 512 + q * 128, 128), 128)
            tile = jnp.concatenate([decw[0, :, cols], dwn[:, cols]], axis=0).T
            for o in range(2):
                wt[0, i, 2 * q + o] = tile[o * 64 : o * 64 + 32]
                wt[1, 2 * q + o, i] = tile[o * 64 + 32 : o * 64 + 64]
        return carry

    def during_inputs(k):
        if k == -2:
            load_d.wait()
            pl.when(has_down)(send_w.start)
            sums[...] = jnp.zeros_like(sums)
            active[...] = jnp.zeros_like(active)
        elif k == -1:
            for load in (load_e, load_t, load_b, load_c):
                load.wait()
            lax.fori_loop(0, 8, sort_encoder, 0)
        else:
            acc = active[...]
            for i in at_distance(k):
                for role in range(2):
                    c, r = colour[role], ring[role][i]
                    acc = acc + dot(encp[c, r], gin[c, r].reshape(512, 128))
            active[...] = acc
        if k == LEVELS[0][0]:
            pl.when(has_up)(send_w.wait_recv)

            @pl.when(jnp.logical_not(has_up))
            def _():
                dwn[...] = jnp.zeros_like(dwn)
                err[pl.ds(64, 64), :] = jnp.zeros((64, 128), BF16)

        if k in LEVELS[0][:3]:
            turn = 3 * LEVELS[0].index(k)
            lax.fori_loop(turn, min(turn + 3, 8), turn_decoders, 0)

    def sort_decoders(i, carry):
        for c in range(2):
            wp[c, i] = wt[c, i].reshape(256, 128).T
        return carry

    def during_codes(k):
        if k == -1:
            lax.fori_loop(0, 8, sort_decoders, 0)
        elif k >= 0:
            acc = sums[...]
            for i in at_distance(k):
                for role in range(2):
                    c, r = colour[role], ring[role][i]
                    acc = acc + dot(wp[c, r], cod[c, r].reshape(256, 128))
            sums[...] = acc

    gather(gin, 0, in_hbm, during_inputs)
    gather_rest(gin, 0, during_inputs)

    pre = active[...] + column(encb_ref[...])
    act = jnp.maximum(pre, 0.0)
    active[...] = act
    cown[...] = (act * act).astype(BF16)
    gather(cod, 1, cown, during_codes)
    gather_rest(cod, 1, during_codes)

    send_r = remote(sums.at[pl.ds(64, 64)], rprev, s_sec.at[1], r_sec.at[1], up)
    send_c = remote(cod, cprev, s_sec.at[2], r_sec.at[2], up)
    send_e = remote(err.at[pl.ds(0, 64)], err.at[pl.ds(64, 64)], s_sec.at[3], r_sec.at[3], down)

    @pl.when(has_up)
    def _():
        send_r.start()
        send_c.start()

    @pl.when(jnp.logical_not(has_down))
    def _():
        rprev[...] = jnp.zeros_like(rprev)

    total = sums[pl.ds(0, 64), :] + column(decb_ref[...])

    @pl.when(has_down)
    def _():
        send_r.wait_recv()

    total = total + rprev[...]
    err[pl.ds(0, 64), :] = ((total - tgt[...].astype(F32)) * scale).astype(BF16)

    @pl.when(has_down)
    def _():
        send_e.start()

    def decoder_grad(slot, codes):
        def step(i, carry):
            block = dot_nt(err[pl.ds(0, 64), :], rows_of(codes, i))
            dg_ref[slot, :, pl.ds(pl.multiple_of(i * 512, 512), 512)] = block.astype(BF16)
            return carry

        lax.fori_loop(0, NY, step, 0)

    decoder_grad(0, cod)
    out_0 = pltpu.make_async_copy(dg_ref.at[0], dg_hbm.at[0], out_sem.at[0])
    out_0.start()

    @pl.when(has_up)
    def _():
        send_e.wait_recv()

    def grad_slabs(m):
        for i in at_distance(m):
            for c, r in ((0, ys[i]), (1, zs[i])):
                part[c, r] = dot(wt[c, r].reshape(256, 128), err[...]).reshape(8, 32, 128)

    def half(h):
        return pl.ds(4 * h, 4)

    def own_part(c, i, h):
        return part[c, ys[i] if c == 0 else zs[i], half(h)]

    def send_sum(c, d, k, h, value):
        way = 1 if d == 0 else -1
        step = way if k in (1, 3) else 2 * way
        to = at(ys[step], z, xl) if c == 0 else at(y, zs[step], xl)
        ring_out[c, d, k - 1, half(h)] = value.astype(BF16)
        remote(
            ring_out.at[c, d, k - 1, half(h)], ring_in.at[c, d, k - 1, half(h)], s_red, r_red.at[c, d, k - 1, h], to
        ).start()

    def got_sum(c, d, k, h):
        arrived(ring_in.at[c, d, k - 1, half(h)], r_red.at[c, d, k - 1, h])
        return ring_in[c, d, k - 1, half(h)].astype(F32)

    for k in (4, 3, 1):
        grad_slabs(k)
        for c in range(2):
            for h in range(2):
                for d in range(2):
                    if k < 4 or h == d:
                        send_sum(c, d, k, h, own_part(c, k if d == 0 else -k, h))
    grad_slabs(2)
    for h in range(2):
        for c in range(2):
            for d in range(2):
                value = own_part(c, 2 if d == 0 else -2, h) + got_sum(c, d, 3, h)
                if h == d:
                    value = value + got_sum(c, d, 4, h)
                send_sum(c, d, 2, h, value)
    grad_slabs(0)

    for c in range(2):
        for h in range(2):
            value = own_part(c, 0, h)
            for k in (1, 2):
                for d in range(2):
                    value = value + got_sum(c, d, k, h)
            two_out[c, half(h)] = value.astype(BF16)
        for o in reversed(OFFS):
            j = zs[o] if c == 0 else ys[o]
            to = at(y, j, 0) if c == 0 else at(j, z, 1)
            send_two = remote(two_out.at[c, j], two_in.at[xl, z if c == 0 else y], s_two, r_two, to)
            if o != 0:
                send_two.start()
            else:
                pl.when(xl != c)(send_two.start)

    @pl.when(has_down)
    def _():
        send_c.wait_recv()
        decoder_grad(1, cprev)

    @pl.when(jnp.logical_not(has_down))
    def _():
        dg_ref[1] = jnp.zeros((64, 4096), BF16)

    out_1 = pltpu.make_async_copy(dg_ref.at[1], dg_hbm.at[1], out_sem.at[1])
    out_1.start()
    arrived(cprev.at[0, pl.ds(0, 5), pl.ds(0, 3)], r_two)
    mine = two_out[xl, line[0][0]].astype(F32) + two_in[1 - xl, line[0][0]].astype(F32)
    for o in OFFS[1:]:
        for p in range(2):
            mine = mine + two_in[p, line[0][o]].astype(F32)

    pre_grad = (mine * 2.0 * active[...]).astype(BF16)

    def enc_step(i, carry):
        block = dot_nt(pre_grad, rows_of(gin, i))
        cols = pl.ds(pl.multiple_of(i * 1024, 1024), 1024)
        eg_ref[:, cols] = block.astype(BF16)
        pltpu.make_async_copy(eg_ref.at[:, cols], eg_hbm.at[:, cols], out_sem.at[2]).start()
        return carry

    lax.fori_loop(0, NY, enc_step, 0)

    pltpu.make_async_copy(eg_ref, eg_hbm, out_sem.at[2]).wait()
    out_0.wait()
    out_1.wait()
    for g, buf in enumerate((gin, cod)):
        arrived(buf.at[0, pl.ds(0, 5), pl.ds(0, 3)], s_line.at[g])
        arrived(buf.at[:, pl.ds(0, 7)], s_ring.at[g])
    arrived(ring_out.at[:, :, :, pl.ds(0, 7)], s_red)
    arrived(cprev.at[0, pl.ds(0, 5), pl.ds(0, 3)], s_two)

    @pl.when(has_down)
    def _():
        send_w.wait_send()
        send_e.wait_send()

    @pl.when(has_up)
    def _():
        send_r.wait_send()
        send_c.wait_send()


def on_device(inputs, targets, enc_w, enc_b, dec_w, dec_b):
    scale = inputs.shape[1] ** (-0.5)
    vmem = pl.BlockSpec(memory_space=pltpu.VMEM)
    hbm = pl.BlockSpec(memory_space=pltpu.HBM)
    dma = pltpu.SemaphoreType.DMA
    grid = (NX, 8, 8, 32, 128)
    eg, dg = pl.pallas_call(
        functools.partial(kernel, scale),
        out_shape=(
            jax.ShapeDtypeStruct((32, 8192), BF16),
            jax.ShapeDtypeStruct((2, 64, 4096), BF16),
        ),
        in_specs=[hbm] * 6,
        out_specs=(hbm, hbm),
        scratch_shapes=[
            pltpu.VMEM((32, 8192), BF16),
            pltpu.VMEM((2, 64, 4096), BF16),
            dma((3,)),
            pltpu.VMEM((NX, 8, 8, 64, 128), BF16),
            pltpu.VMEM(grid, BF16),
            pltpu.VMEM(grid, BF16),
            pltpu.VMEM((32, 128), BF16),
            pltpu.VMEM((64, 128), BF16),
            pltpu.VMEM((1, 32), F32),
            pltpu.VMEM((1, 64), F32),
            pltpu.VMEM((32, 8192), BF16),
            pltpu.VMEM((2, 64, 4096), BF16),
            pltpu.VMEM((64, 4096), BF16),
            pltpu.VMEM((128, 128), BF16),
            pltpu.VMEM((64, 128), F32),
            pltpu.VMEM((128, 128), F32),
            pltpu.VMEM((NX, 8, 32, 512), BF16),
            pltpu.VMEM(grid, BF16),
            pltpu.VMEM((NX, 8, 128, 256), BF16),
            pltpu.VMEM((32, 128), F32),
            pltpu.VMEM(grid, F32),
            pltpu.VMEM((2, 2, 4, 8, 32, 128), BF16),
            pltpu.VMEM((2, 2, 4, 8, 32, 128), BF16),
            pltpu.VMEM((2, 8, 32, 128), BF16),
            pltpu.VMEM((2, 8, 32, 128), BF16),
            dma((5,)),
            dma((2,)),
            dma((2, 3)),
            dma((2,)),
            dma((2, 2, 2, 4, max(PIECES))),
            dma((4,)),
            dma((4,)),
            dma,
            dma((2, 2, 4, 2)),
            dma,
            dma,
        ],
        compiler_params=pltpu.CompilerParams(collective_id=0, has_side_effects=True),
    )(inputs[0].T, targets[0].T, enc_w[0], enc_b, dec_w[0], dec_b)
    return eg[None], dg[None]


def solution(mesh):
    return jax.shard_map(
        on_device,
        mesh=mesh,
        in_specs=(
            P("section", None, "feat"),
            P("section", None, "feat"),
            P("section", "feat", None),
            P("section", "feat"),
            P("section", None, "feat", None),
            P("section", "feat"),
        ),
        out_specs=(P("section", "feat", None), P("section", None, "feat", None)),
        check_vma=False,
    )
```

```python
import functools

import jax
import jax.numpy as jnp
from jax import lax
from jax.experimental import pallas as pl
from jax.experimental.pallas import tpu as pltpu
from jax.sharding import PartitionSpec as P

MESH = pl.DeviceIdType.MESH
NY, NZ, NX = 8, 8, 2
BF16, F32 = jnp.bfloat16, jnp.float32


def mod(a, n):
    return lax.rem(a + n, n)


def dot(a, b):
    return jnp.dot(a, b, preferred_element_type=F32)


def dot_nt(a, b):
    return lax.dot_general(a, b, (((1,), (1,)), ((), ())), preferred_element_type=F32)


def column(row):
    n = row.shape[1]
    here = lax.broadcasted_iota(jnp.int32, (n, n), 0) == lax.broadcasted_iota(jnp.int32, (n, n), 1)
    return jnp.sum(jnp.where(here, jnp.broadcast_to(row, (n, n)), 0.0), axis=1, keepdims=True)


GROUPS = ((0, 1, -1), (2, -2), (3, -3, 4))
OFFS = tuple(o for group in GROUPS for o in group)


def group_of(o):
    return next(n for n, group in enumerate(GROUPS) if o in group)


def back(o):
    return o if o == 4 else -o


def reach(d, o):
    return 4 if OFFS.index(o) % 2 == d else 3


def travellers(n, d, k):
    return [o for o in GROUPS[n] if k <= reach(d, o)]


PIECES = (2, 2)
LEVELS = (2, 1, 3, 4)


def carries(g, k, h, d):
    return k < 4 or (d == 0 if PIECES[g] == 1 else h // (PIECES[g] // 2) == d)


def kernel(
    scale, in_hbm, tgt_hbm, encw_hbm, encb_hbm, decw_hbm, decb_hbm,
    eg_hbm, dg_hbm,
    eg_ref, dg_ref, out_sem, gin, cod, cprev, cown, tgt, encb_ref, decb_ref, encw, decw, dwn, err, rprev, sums, encp, encr, pre_sum, pre_in, wt, wp, active, part, ring_in, ring_out, two_in, two_out,
    load_sem, s_line, r_one, s_ring, r_ring, s_sec, r_sec, s_red, r_red, s_two, r_two,
):
    s = lax.axis_index("section")
    f = lax.axis_index("feat")
    xl = lax.rem(f, NX)
    z = lax.rem(f // NX, NZ)
    y = f // (NX * NZ)
    ys = {o: mod(y + o, NY) for o in range(-4, 5)}
    zs = {o: mod(z + o, NZ) for o in range(-4, 5)}

    def at(yy, zz, xx):
        return {"section": s, "feat": (yy * NZ + zz) * NX + xx}

    far_f = (y * NZ + z) * NX + 1 - xl
    odd = lax.rem(s, 2)
    up = {"section": jnp.minimum(s + 1, 3), "feat": jnp.where(odd == 1, far_f, f)}
    down = {"section": jnp.maximum(s - 1, 0), "feat": jnp.where(odd == 0, far_f, f)}
    has_up = s < 3
    has_down = s > 0

    even = xl == 0
    ring = [{o: jnp.where(even, ys[o], zs[o]) for o in ys}, {o: jnp.where(even, zs[o], ys[o]) for o in ys}]
    line = ring[::-1]
    colour = [xl, 1 - xl]

    def along_ring(role, o, xx):
        if role == 0:
            return at(jnp.where(even, ys[o], y), jnp.where(even, z, zs[o]), xx)
        return at(jnp.where(even, y, ys[o]), jnp.where(even, zs[o], z), xx)

    mate = at(y, z, 1 - xl)
    barrier = pltpu.get_barrier_semaphore()
    for o in OFFS:
        if o != 0:
            pl.semaphore_signal(barrier, inc=1, device_id=at(ys[o], z, xl), device_id_type=MESH)
            pl.semaphore_signal(barrier, inc=1, device_id=at(y, zs[o], xl), device_id_type=MESH)
        pl.semaphore_signal(barrier, inc=1, device_id=along_ring(1, o, 1 - xl), device_id_type=MESH)
        if o != 0:
            pl.semaphore_signal(barrier, inc=1, device_id=along_ring(0, o, 1 - xl), device_id_type=MESH)

    @pl.when(has_up)
    def _():
        pl.semaphore_signal(barrier, inc=1, device_id=up, device_id_type=MESH)

    @pl.when(has_down)
    def _():
        pl.semaphore_signal(barrier, inc=1, device_id=down, device_id_type=MESH)

    load_e = pltpu.make_async_copy(encw_hbm, encw, load_sem.at[0])
    load_d = pltpu.make_async_copy(decw_hbm, decw, load_sem.at[1])
    load_t = pltpu.make_async_copy(tgt_hbm, tgt, load_sem.at[2])
    load_b = pltpu.make_async_copy(encb_hbm, encb_ref, load_sem.at[3])
    load_c = pltpu.make_async_copy(decb_hbm, decb_ref, load_sem.at[4])
    for load in (load_d, load_e, load_t, load_b, load_c):
        load.start()

    pl.semaphore_wait(barrier, 29 + jnp.where(has_up, 1, 0) + jnp.where(has_down, 1, 0))

    def remote(src, dst, ss, rs, to):
        return pltpu.make_async_remote_copy(
            src_ref=src, dst_ref=dst, send_sem=ss, recv_sem=rs, device_id=to, device_id_type=MESH
        )

    def arrived(blocks, sem):
        pltpu.make_async_copy(blocks, blocks, sem).wait()

    def place(buf, g, role, i, o):
        if g == 0:
            return buf.at[role, (ys, zs)[role][i], (zs, ys)[role][o]]
        return buf.at[colour[role], ring[role][i], line[role][o]]

    def along(g, role, o, xx):
        if g == 1:
            return along_ring(role, o, xx)
        return at(ys[o], z, xx) if role == 0 else at(y, zs[o], xx)

    def gather(buf, g, sources):
        for role, src in enumerate(sources):
            own = place(buf, g, role, 0, 0)
            pltpu.make_async_copy(src, own, r_one.at[g, role]).start()
            for o in reversed(OFFS):
                if g == 1:
                    remote(src, own, s_line.at[g], r_one.at[g, 1], along(g, 1, o, 1 - xl)).start()
                if o != 0:
                    remote(src, own, s_line.at[g], r_one.at[g, role], along(g, 1 - role, o, xl)).start()

    def gather_rest(buf, g, meanwhile):
        meanwhile(-1)
        blocks = 8 // PIECES[g]

        def piece(role, i, h):
            c, at_ring = (role, (ys, zs)[role]) if g == 0 else (colour[role], ring[role])
            return buf.at[c, at_ring[i], pl.ds(h * blocks, blocks)]

        def send(role, d, k, h):
            way = 1 if d == 0 else -1
            ref = piece(role, 0 if k < 3 else -2 * way, h)
            to = along(g, role, way if k in (1, 3) else 2 * way, xl)
            remote(ref, ref, s_ring.at[g], r_ring.at[g, role, d, k - 1, h], to).start()

        for role in range(2):
            arrived(buf.at[0, 0], r_one.at[g, role])
            for k in (2, 1):
                for h in range(PIECES[g]):
                    for d in range(2):
                        send(role, d, k, h)
        meanwhile(0)
        for k in LEVELS:
            for h in range(PIECES[g]):
                for role in range(2):
                    for d in range(2):
                        if carries(g, k, h, d):
                            arrived(piece(role, -k if d == 0 else k, h), r_ring.at[g, role, d, k - 1, h])
                        if k == 2:
                            for further in (4, 3):
                                if carries(g, further, h, d):
                                    send(role, d, further, h)
            meanwhile(k)

    def rows_of(buf, i):
        return jnp.stack([buf[0, i], buf[1, :, i]], axis=1).reshape(-1, 128)

    def input_rows(i):
        parts = [gin[c, 0, i] if r == 0 else gin[c, 1, :, i] for c in range(2) for r in range(2)]
        return jnp.stack(parts, axis=1).reshape(-1, 128)

    send_w = remote(decw.at[1], dwn, s_sec.at[0], r_sec.at[0], down)

    def at_distance(k):
        return (k,) if k in (0, 4) else (k, -k)

    def sort_encoder(i, carry):
        for c in range(2):
            for r in range(2):
                for j in range(2):
                    parts = []
                    for o in range(4 * j, 4 * j + 4):
                        base = i * 1024 + o * 128 if r == 0 else o * 1024 + i * 128
                        first = c * 64 + r * 32
                        parts.append(encw[:, pl.ds(pl.multiple_of(base, 128), 128)][:, first : first + 32])
                    encp[c, r, i, :, j * 128 : j * 128 + 128] = jnp.concatenate(parts, axis=1)
        return carry

    def turn_decoders(i, carry):
        for q in range(4):
            cols = pl.ds(pl.multiple_of(i * 512 + q * 128, 128), 128)
            tile = jnp.concatenate([decw[0, :, cols], dwn[:, cols]], axis=0).T
            for o in range(2):
                wt[0, i, 2 * q + o] = tile[o * 64 : o * 64 + 32]
                wt[1, 2 * q + o, i] = tile[o * 64 + 32 : o * 64 + 64]
        return carry

    send_p = remote(encp.at[1 - xl], encr, s_sec.at[4], r_sec.at[4], mate)
    send_s = remote(pre_sum.at[pl.ds(32, 32)], pre_in, s_sec.at[5], r_sec.at[5], mate)
    send_g = remote(gin.at[xl], gin.at[xl], s_sec.at[6], r_sec.at[6], mate)

    def during_inputs(k):
        if k == -1:
            load_d.wait()
            pl.when(has_down)(send_w.start)
            sums[...] = jnp.zeros_like(sums)
            pre_sum[...] = jnp.zeros_like(pre_sum)
            for load in (load_e, load_t, load_b, load_c):
                load.wait()
            lax.fori_loop(0, 8, sort_encoder, 0)
            send_p.start()
        elif k > 0:
            if k == LEVELS[0]:
                send_p.wait_recv()
            acc = pre_sum[...]
            for i in at_distance(k) + (at_distance(0) if k == LEVELS[0] else ()):
                for role in range(2):
                    r = (ys, zs)[role][i]
                    both = jnp.concatenate([encp[xl, role, r], encr[role, r]], axis=0)
                    acc = acc + dot(both, gin[xl, role, r].reshape(256, 128))
            pre_sum[...] = acc
        if k == LEVELS[0]:
            pl.when(has_up)(send_w.wait_recv)

            @pl.when(jnp.logical_not(has_up))
            def _():
                dwn[...] = jnp.zeros_like(dwn)
                err[pl.ds(64, 64), :] = jnp.zeros((64, 128), BF16)

        if k in LEVELS[:3]:
            turn = 3 * LEVELS.index(k)
            lax.fori_loop(turn, min(turn + 3, 8), turn_decoders, 0)

    def sort_decoders(i, carry):
        for c in range(2):
            wp[c, i] = wt[c, i].reshape(256, 128).T
        return carry

    def during_codes(k):
        if k == -1:
            lax.fori_loop(0, 8, sort_decoders, 0)
        elif k >= 0:
            if k == 0:
                send_g.start()
            acc = sums[...]
            for i in at_distance(k):
                for role in range(2):
                    c, r = colour[role], ring[role][i]
                    acc = acc + dot(wp[c, r], cod[c, r].reshape(256, 128))
            sums[...] = acc

    gather(gin.at[xl], 0, (in_hbm.at[pl.ds(0, 32)], in_hbm.at[pl.ds(32, 32)]))
    gather_rest(gin.at[xl], 0, during_inputs)

    send_s.start()
    send_s.wait_recv()
    pre = pre_sum[pl.ds(0, 32), :] + pre_in[...] + column(encb_ref[...])
    act = jnp.maximum(pre, 0.0)
    active[...] = act
    cown[...] = (act * act).astype(BF16)
    gather(cod, 1, (cown,))
    gather_rest(cod, 1, during_codes)

    send_r = remote(sums.at[pl.ds(64, 64)], rprev, s_sec.at[1], r_sec.at[1], up)
    send_c = remote(cod, cprev, s_sec.at[2], r_sec.at[2], up)
    send_e = remote(err.at[pl.ds(0, 64)], err.at[pl.ds(64, 64)], s_sec.at[3], r_sec.at[3], down)

    @pl.when(has_up)
    def _():
        send_r.start()
        send_c.start()

    @pl.when(jnp.logical_not(has_down))
    def _():
        rprev[...] = jnp.zeros_like(rprev)

    total = sums[pl.ds(0, 64), :] + column(decb_ref[...])

    @pl.when(has_down)
    def _():
        send_r.wait_recv()

    total = total + rprev[...]
    err[pl.ds(0, 64), :] = ((total - tgt[...].astype(F32)) * scale).astype(BF16)

    @pl.when(has_down)
    def _():
        send_e.start()

    def decoder_grad(slot, codes):
        def step(i, carry):
            block = dot_nt(err[pl.ds(0, 64), :], rows_of(codes, i))
            dg_ref[slot, :, pl.ds(pl.multiple_of(i * 512, 512), 512)] = block.astype(BF16)
            return carry

        lax.fori_loop(0, NY, step, 0)

    decoder_grad(0, cod)
    out_0 = pltpu.make_async_copy(dg_ref.at[0], dg_hbm.at[0], out_sem.at[0])
    out_0.start()

    @pl.when(has_up)
    def _():
        send_e.wait_recv()

    def grad_slabs(m):
        for i in at_distance(m):
            for c, r in ((0, ys[i]), (1, zs[i])):
                part[c, r] = dot(wt[c, r].reshape(256, 128), err[...]).reshape(8, 32, 128)

    def half(h):
        return pl.ds(4 * h, 4)

    def own_part(c, i, h):
        return part[c, ys[i] if c == 0 else zs[i], half(h)]

    def send_sum(c, d, k, h, value):
        way = 1 if d == 0 else -1
        step = way if k in (1, 3) else 2 * way
        to = at(ys[step], z, xl) if c == 0 else at(y, zs[step], xl)
        ring_out[c, d, k - 1, half(h)] = value.astype(BF16)
        remote(
            ring_out.at[c, d, k - 1, half(h)], ring_in.at[c, d, k - 1, half(h)], s_red, r_red.at[c, d, k - 1, h], to
        ).start()

    def got_sum(c, d, k, h):
        arrived(ring_in.at[c, d, k - 1, half(h)], r_red.at[c, d, k - 1, h])
        return ring_in[c, d, k - 1, half(h)].astype(F32)

    for k in (4, 3, 1):
        grad_slabs(k)
        for c in range(2):
            for h in range(2):
                for d in range(2):
                    if k < 4 or h == d:
                        send_sum(c, d, k, h, own_part(c, k if d == 0 else -k, h))
    grad_slabs(2)
    for h in range(2):
        for c in range(2):
            for d in range(2):
                value = own_part(c, 2 if d == 0 else -2, h) + got_sum(c, d, 3, h)
                if h == d:
                    value = value + got_sum(c, d, 4, h)
                send_sum(c, d, 2, h, value)
    grad_slabs(0)

    for c in range(2):
        for h in range(2):
            value = own_part(c, 0, h)
            for k in (1, 2):
                for d in range(2):
                    value = value + got_sum(c, d, k, h)
            two_out[c, half(h)] = value.astype(BF16)
        for o in reversed(OFFS):
            j = zs[o] if c == 0 else ys[o]
            to = at(y, j, 0) if c == 0 else at(j, z, 1)
            send_two = remote(two_out.at[c, j], two_in.at[xl, z if c == 0 else y], s_two, r_two, to)
            if o != 0:
                send_two.start()
            else:
                pl.when(xl != c)(send_two.start)

    @pl.when(has_down)
    def _():
        send_c.wait_recv()
        decoder_grad(1, cprev)

    @pl.when(jnp.logical_not(has_down))
    def _():
        dg_ref[1] = jnp.zeros((64, 4096), BF16)

    out_1 = pltpu.make_async_copy(dg_ref.at[1], dg_hbm.at[1], out_sem.at[1])
    out_1.start()
    arrived(cprev.at[0, pl.ds(0, 5), pl.ds(0, 3)], r_two)
    mine = two_out[xl, line[0][0]].astype(F32) + two_in[1 - xl, line[0][0]].astype(F32)
    for o in OFFS[1:]:
        for p in range(2):
            mine = mine + two_in[p, line[0][o]].astype(F32)

    send_g.wait_recv()
    pre_grad = (mine * 2.0 * active[...]).astype(BF16)

    def enc_step(i, carry):
        block = dot_nt(pre_grad, input_rows(i))
        cols = pl.ds(pl.multiple_of(i * 1024, 1024), 1024)
        eg_ref[:, cols] = block.astype(BF16)
        pltpu.make_async_copy(eg_ref.at[:, cols], eg_hbm.at[:, cols], out_sem.at[2]).start()
        return carry

    lax.fori_loop(0, NY, enc_step, 0)

    pltpu.make_async_copy(eg_ref, eg_hbm, out_sem.at[2]).wait()
    out_0.wait()
    out_1.wait()
    arrived(cod.at[:, 0, pl.ds(0, 7)], s_line.at[0])
    arrived(cod.at[0, pl.ds(0, 5), pl.ds(0, 3)], s_line.at[1])
    for g in range(2):
        arrived(cod.at[:, pl.ds(0, 7)], s_ring.at[g])
    for copy in (send_p, send_s, send_g):
        copy.wait_send()
    arrived(ring_out.at[:, :, :, pl.ds(0, 7)], s_red)
    arrived(cprev.at[0, pl.ds(0, 5), pl.ds(0, 3)], s_two)

    @pl.when(has_down)
    def _():
        send_w.wait_send()
        send_e.wait_send()

    @pl.when(has_up)
    def _():
        send_r.wait_send()
        send_c.wait_send()


def on_device(inputs, targets, enc_w, enc_b, dec_w, dec_b):
    scale = inputs.shape[1] ** (-0.5)
    vmem = pl.BlockSpec(memory_space=pltpu.VMEM)
    hbm = pl.BlockSpec(memory_space=pltpu.HBM)
    dma = pltpu.SemaphoreType.DMA
    grid = (NX, 8, 8, 32, 128)
    eg, dg = pl.pallas_call(
        functools.partial(kernel, scale),
        out_shape=(
            jax.ShapeDtypeStruct((32, 8192), BF16),
            jax.ShapeDtypeStruct((2, 64, 4096), BF16),
        ),
        in_specs=[hbm] * 6,
        out_specs=(hbm, hbm),
        scratch_shapes=[
            pltpu.VMEM((32, 8192), BF16),
            pltpu.VMEM((2, 64, 4096), BF16),
            dma((3,)),
            pltpu.VMEM((NX, NX, 8, 8, 32, 128), BF16),
            pltpu.VMEM(grid, BF16),
            pltpu.VMEM(grid, BF16),
            pltpu.VMEM((32, 128), BF16),
            pltpu.VMEM((64, 128), BF16),
            pltpu.VMEM((1, 32), F32),
            pltpu.VMEM((1, 64), F32),
            pltpu.VMEM((32, 8192), BF16),
            pltpu.VMEM((2, 64, 4096), BF16),
            pltpu.VMEM((64, 4096), BF16),
            pltpu.VMEM((128, 128), BF16),
            pltpu.VMEM((64, 128), F32),
            pltpu.VMEM((128, 128), F32),
            pltpu.VMEM((NX, NX, 8, 32, 256), BF16),
            pltpu.VMEM((NX, 8, 32, 256), BF16),
            pltpu.VMEM((64, 128), F32),
            pltpu.VMEM((32, 128), F32),
            pltpu.VMEM(grid, BF16),
            pltpu.VMEM((NX, 8, 128, 256), BF16),
            pltpu.VMEM((32, 128), F32),
            pltpu.VMEM(grid, F32),
            pltpu.VMEM((2, 2, 4, 8, 32, 128), BF16),
            pltpu.VMEM((2, 2, 4, 8, 32, 128), BF16),
            pltpu.VMEM((2, 8, 32, 128), BF16),
            pltpu.VMEM((2, 8, 32, 128), BF16),
            dma((5,)),
            dma((2,)),
            dma((2, 2)),
            dma((2,)),
            dma((2, 2, 2, 4, max(PIECES))),
            dma((7,)),
            dma((7,)),
            dma,
            dma((2, 2, 4, 2)),
            dma,
            dma,
        ],
        compiler_params=pltpu.CompilerParams(collective_id=0, has_side_effects=True),
    )(inputs[0].T, targets[0].T, enc_w[0], enc_b, dec_w[0], dec_b)
    return eg[None], dg[None]


def solution(mesh):
    return jax.shard_map(
        on_device,
        mesh=mesh,
        in_specs=(
            P("section", None, "feat"),
            P("section", None, "feat"),
            P("section", "feat", None),
            P("section", "feat"),
            P("section", None, "feat", None),
            P("section", "feat"),
        ),
        out_specs=(P("section", "feat", None), P("section", None, "feat", None)),
        check_vma=False,
    )
```

```python
import functools

import jax
import jax.numpy as jnp
from jax import lax
from jax.experimental import pallas as pl
from jax.experimental.pallas import tpu as pltpu
from jax.sharding import PartitionSpec as P

MESH = pl.DeviceIdType.MESH
NY, NZ, NX = 8, 8, 2
BF16, F32 = jnp.bfloat16, jnp.float32


def mod(a, n):
    return lax.rem(a + n, n)


def dot(a, b):
    return jnp.dot(a, b, preferred_element_type=F32)


def dot_nt(a, b):
    return lax.dot_general(a, b, (((1,), (1,)), ((), ())), preferred_element_type=F32)


def column(row):
    n = row.shape[1]
    here = lax.broadcasted_iota(jnp.int32, (n, n), 0) == lax.broadcasted_iota(jnp.int32, (n, n), 1)
    return jnp.sum(jnp.where(here, jnp.broadcast_to(row, (n, n)), 0.0), axis=1, keepdims=True)


GROUPS = ((0, 1, -1), (2, -2), (3, -3, 4))
OFFS = tuple(o for group in GROUPS for o in group)


def group_of(o):
    return next(n for n, group in enumerate(GROUPS) if o in group)


def back(o):
    return o if o == 4 else -o


def reach(d, o):
    return 4 if OFFS.index(o) % 2 == d else 3


def travellers(n, d, k):
    return [o for o in GROUPS[n] if k <= reach(d, o)]


PIECES = (2, 2)
LEVELS = (2, 1, 3, 4)


def sem_of(k, h, split):
    return h if k == split else 2 + [n for n in (1, 2, 3, 4) if n != split].index(k)


def carries(g, k, h, d):
    return k < 4 or (d == 0 if PIECES[g] == 1 else h // (PIECES[g] // 2) == d)


def kernel(
    scale, in_hbm, tgt_hbm, encw_hbm, encb_hbm, decw_hbm, decb_hbm,
    eg_hbm, dg_hbm,
    eg_ref, dg_ref, out_sem, gin, cod, cprev, cown, tgt, encb_ref, decb_ref, encw, decw, dwn, err, rprev, sums, encp, encr, pre_sum, pre_in, wt, wp, active, part, ring_in, ring_out, two_in, two_out,
    load_sem, s_line, r_one, s_ring, r_ring, s_sec, r_sec, s_red, r_red, s_two, r_two,
):
    s = lax.axis_index("section")
    f = lax.axis_index("feat")
    xl = lax.rem(f, NX)
    z = lax.rem(f // NX, NZ)
    y = f // (NX * NZ)
    ys = {o: mod(y + o, NY) for o in range(-4, 5)}
    zs = {o: mod(z + o, NZ) for o in range(-4, 5)}

    def at(yy, zz, xx):
        return {"section": s, "feat": (yy * NZ + zz) * NX + xx}

    far_f = (y * NZ + z) * NX + 1 - xl
    odd = lax.rem(s, 2)
    up = {"section": jnp.minimum(s + 1, 3), "feat": jnp.where(odd == 1, far_f, f)}
    down = {"section": jnp.maximum(s - 1, 0), "feat": jnp.where(odd == 0, far_f, f)}
    has_up = s < 3
    has_down = s > 0

    even = xl == 0
    ring = [{o: jnp.where(even, ys[o], zs[o]) for o in ys}, {o: jnp.where(even, zs[o], ys[o]) for o in ys}]
    line = ring[::-1]
    colour = [xl, 1 - xl]

    def along_ring(role, o, xx):
        if role == 0:
            return at(jnp.where(even, ys[o], y), jnp.where(even, z, zs[o]), xx)
        return at(jnp.where(even, y, ys[o]), jnp.where(even, zs[o], z), xx)

    mate = at(y, z, 1 - xl)
    barrier = pltpu.get_barrier_semaphore()
    for o in OFFS:
        if o != 0:
            pl.semaphore_signal(barrier, inc=1, device_id=at(ys[o], z, xl), device_id_type=MESH)
            pl.semaphore_signal(barrier, inc=1, device_id=at(y, zs[o], xl), device_id_type=MESH)
        pl.semaphore_signal(barrier, inc=1, device_id=along_ring(1, o, 1 - xl), device_id_type=MESH)
        if o != 0:
            pl.semaphore_signal(barrier, inc=1, device_id=along_ring(0, o, 1 - xl), device_id_type=MESH)

    @pl.when(has_up)
    def _():
        pl.semaphore_signal(barrier, inc=1, device_id=up, device_id_type=MESH)

    @pl.when(has_down)
    def _():
        pl.semaphore_signal(barrier, inc=1, device_id=down, device_id_type=MESH)

    load_e = pltpu.make_async_copy(encw_hbm, encw, load_sem.at[0])
    load_d = pltpu.make_async_copy(decw_hbm, decw, load_sem.at[1])
    load_t = pltpu.make_async_copy(tgt_hbm, tgt, load_sem.at[2])
    load_b = pltpu.make_async_copy(encb_hbm, encb_ref, load_sem.at[3])
    load_c = pltpu.make_async_copy(decb_hbm, decb_ref, load_sem.at[4])
    for load in (load_d, load_e, load_t, load_b, load_c):
        load.start()

    pl.semaphore_wait(barrier, 29 + jnp.where(has_up, 1, 0) + jnp.where(has_down, 1, 0))

    def remote(src, dst, ss, rs, to):
        return pltpu.make_async_remote_copy(
            src_ref=src, dst_ref=dst, send_sem=ss, recv_sem=rs, device_id=to, device_id_type=MESH
        )

    def arrived(blocks, sem):
        pltpu.make_async_copy(blocks, blocks, sem).wait()

    def place(buf, g, role, i, o):
        if g == 0:
            return buf.at[role, (ys, zs)[role][i], (zs, ys)[role][o]]
        return buf.at[colour[role], ring[role][i], line[role][o]]

    def along(g, role, o, xx):
        if g == 1:
            return along_ring(role, o, xx)
        return at(ys[o], z, xx) if role == 0 else at(y, zs[o], xx)

    def gather(buf, g, sources):
        for role, src in enumerate(sources):
            own = place(buf, g, role, 0, 0)
            pltpu.make_async_copy(src, own, r_one.at[g, role]).start()
            for o in reversed(OFFS):
                if g == 1:
                    remote(src, own, s_line.at[g], r_one.at[g, 1], along(g, 1, o, 1 - xl)).start()
                if o != 0:
                    remote(src, own, s_line.at[g], r_one.at[g, role], along(g, 1 - role, o, xl)).start()

    def gather_rest(buf, g, meanwhile):
        meanwhile(-1)
        blocks = 8 // PIECES[g]

        def piece(role, i, h):
            c, at_ring = (role, (ys, zs)[role]) if g == 0 else (colour[role], ring[role])
            return buf.at[c, at_ring[i], pl.ds(h * blocks, blocks)]

        def send(role, d, k, h):
            way = 1 if d == 0 else -1
            ref = piece(role, 0 if k < 3 else -2 * way, h)
            to = along(g, role, way if k in (1, 3) else 2 * way, xl)
            remote(ref, ref, s_ring.at[g], r_ring.at[g, role, d, sem_of(k, h, 2)], to).start()

        for role in range(2):
            arrived(buf.at[0, 0], r_one.at[g, role])
            for k in (2, 1):
                for h in range(PIECES[g]):
                    for d in range(2):
                        send(role, d, k, h)
        meanwhile(0)
        for k in LEVELS:
            for h in range(PIECES[g]):
                for role in range(2):
                    for d in range(2):
                        i = -k if d == 0 else k
                        if k in (2, 4) and carries(g, k, h, d):
                            arrived(piece(role, i, h), r_ring.at[g, role, d, sem_of(k, h, 2)])
                        elif k in (1, 3) and h == 0:
                            arrived(buf.at[0, 0], r_ring.at[g, role, d, sem_of(k, h, 2)])
                        if k == 2:
                            for further in (4, 3):
                                if carries(g, further, h, d):
                                    send(role, d, further, h)
            meanwhile(k)

    def rows_of(buf, i):
        return jnp.stack([buf[0, i], buf[1, :, i]], axis=1).reshape(-1, 128)

    def input_rows(i):
        parts = [gin[c, 0, i] if r == 0 else gin[c, 1, :, i] for c in range(2) for r in range(2)]
        return jnp.stack(parts, axis=1).reshape(-1, 128)

    send_w = remote(decw.at[1], dwn, s_sec.at[0], r_sec.at[0], down)

    def at_distance(k):
        return (k,) if k in (0, 4) else (k, -k)

    def sort_encoder(i, carry):
        for c in range(2):
            for r in range(2):
                for j in range(2):
                    parts = []
                    for o in range(4 * j, 4 * j + 4):
                        base = i * 1024 + o * 128 if r == 0 else o * 1024 + i * 128
                        first = c * 64 + r * 32
                        parts.append(encw[:, pl.ds(pl.multiple_of(base, 128), 128)][:, first : first + 32])
                    encp[c, r, i, :, j * 128 : j * 128 + 128] = jnp.concatenate(parts, axis=1)
        return carry

    def turn_decoders(i, carry):
        for q in range(4):
            cols = pl.ds(pl.multiple_of(i * 512 + q * 128, 128), 128)
            tile = jnp.concatenate([decw[0, :, cols], dwn[:, cols]], axis=0).T
            for o in range(2):
                wt[0, i, 2 * q + o] = tile[o * 64 : o * 64 + 32]
                wt[1, 2 * q + o, i] = tile[o * 64 + 32 : o * 64 + 64]
        return carry

    send_p = remote(encp.at[1 - xl], encr, s_sec.at[4], r_sec.at[4], mate)
    send_s = remote(pre_sum.at[pl.ds(32, 32)], pre_in, s_sec.at[5], r_sec.at[5], mate)
    send_g = remote(gin.at[xl], gin.at[xl], s_sec.at[6], r_sec.at[6], mate)

    def during_inputs(k):
        if k == -1:
            load_d.wait()
            pl.when(has_down)(send_w.start)
            sums[...] = jnp.zeros_like(sums)
            pre_sum[...] = jnp.zeros_like(pre_sum)
            for load in (load_e, load_t, load_b, load_c):
                load.wait()
            lax.fori_loop(0, 8, sort_encoder, 0)
            send_p.start()
        elif k > 0:
            if k == LEVELS[0]:
                send_p.wait_recv()
            acc = pre_sum[...]
            for i in at_distance(k) + (at_distance(0) if k == LEVELS[0] else ()):
                for role in range(2):
                    r = (ys, zs)[role][i]
                    both = jnp.concatenate([encp[xl, role, r], encr[role, r]], axis=0)
                    acc = acc + dot(both, gin[xl, role, r].reshape(256, 128))
            pre_sum[...] = acc
        if k == LEVELS[0]:
            pl.when(has_up)(send_w.wait_recv)

            @pl.when(jnp.logical_not(has_up))
            def _():
                dwn[...] = jnp.zeros_like(dwn)
                err[pl.ds(64, 64), :] = jnp.zeros((64, 128), BF16)

        if k in LEVELS[:3]:
            turn = 3 * LEVELS.index(k)
            lax.fori_loop(turn, min(turn + 3, 8), turn_decoders, 0)

    def sort_decoders(i, carry):
        for c in range(2):
            wp[c, i] = wt[c, i].reshape(256, 128).T
        return carry

    def during_codes(k):
        if k == -1:
            lax.fori_loop(0, 8, sort_decoders, 0)
        elif k >= 0:
            if k == 0:
                send_g.start()
            acc = sums[...]
            for i in at_distance(k):
                for role in range(2):
                    c, r = colour[role], ring[role][i]
                    acc = acc + dot(wp[c, r], cod[c, r].reshape(256, 128))
            sums[...] = acc

    gather(gin.at[xl], 0, (in_hbm.at[pl.ds(0, 32)], in_hbm.at[pl.ds(32, 32)]))
    gather_rest(gin.at[xl], 0, during_inputs)

    send_s.start()
    pre = pre_sum[pl.ds(0, 32), :] + column(encb_ref[...])
    send_s.wait_recv()
    pre = pre + pre_in[...]
    act = jnp.maximum(pre, 0.0)
    active[...] = act
    cown[...] = (act * act).astype(BF16)
    gather(cod, 1, (cown,))
    gather_rest(cod, 1, during_codes)

    send_r = remote(sums.at[pl.ds(64, 64)], rprev, s_sec.at[1], r_sec.at[1], up)
    send_c = remote(cod, cprev, s_sec.at[2], r_sec.at[2], up)
    send_e = remote(err.at[pl.ds(0, 64)], err.at[pl.ds(64, 64)], s_sec.at[3], r_sec.at[3], down)

    @pl.when(has_up)
    def _():
        send_r.start()
        send_c.start()

    @pl.when(jnp.logical_not(has_down))
    def _():
        rprev[...] = jnp.zeros_like(rprev)

    total = sums[pl.ds(0, 64), :] + column(decb_ref[...])

    @pl.when(has_down)
    def _():
        send_r.wait_recv()

    total = total + rprev[...]
    err[pl.ds(0, 64), :] = ((total - tgt[...].astype(F32)) * scale).astype(BF16)

    @pl.when(has_down)
    def _():
        send_e.start()

    def decoder_grad(slot, codes):
        def step(i, carry):
            block = dot_nt(err[pl.ds(0, 64), :], rows_of(codes, i))
            dg_ref[slot, :, pl.ds(pl.multiple_of(i * 512, 512), 512)] = block.astype(BF16)
            return carry

        lax.fori_loop(0, NY, step, 0)

    decoder_grad(0, cod)
    out_0 = pltpu.make_async_copy(dg_ref.at[0], dg_hbm.at[0], out_sem.at[0])
    out_0.start()

    @pl.when(has_up)
    def _():
        send_e.wait_recv()

    def grad_slabs(m):
        for i in at_distance(m):
            for c, r in ((0, ys[i]), (1, zs[i])):
                part[c, r] = dot(wt[c, r].reshape(256, 128), err[...]).reshape(8, 32, 128)

    def half(h):
        return pl.ds(4 * h, 4)

    def own_part(c, i, h):
        return part[c, ys[i] if c == 0 else zs[i], half(h)]

    def send_sum(c, d, k, h, value):
        way = 1 if d == 0 else -1
        step = way if k in (1, 3) else 2 * way
        to = at(ys[step], z, xl) if c == 0 else at(y, zs[step], xl)
        ring_out[c, d, k - 1, half(h)] = value.astype(BF16)
        remote(
            ring_out.at[c, d, k - 1, half(h)], ring_in.at[c, d, k - 1, half(h)], s_red, r_red.at[c, d, sem_of(k, h, 3)], to
        ).start()

    def got_sum(c, d, k, h):
        if k > 2:
            arrived(ring_in.at[c, d, k - 1, half(h)], r_red.at[c, d, sem_of(k, h, 3)])
        elif h == 0:
            arrived(ring_in.at[c, d, k - 1], r_red.at[c, d, sem_of(k, h, 3)])
        return ring_in[c, d, k - 1, half(h)].astype(F32)

    for k in (4, 3, 1):
        grad_slabs(k)
        for c in range(2):
            for h in range(2):
                for d in range(2):
                    if k < 4 or h == d:
                        send_sum(c, d, k, h, own_part(c, k if d == 0 else -k, h))
    grad_slabs(2)
    for h in range(2):
        for c in range(2):
            for d in range(2):
                value = own_part(c, 2 if d == 0 else -2, h) + got_sum(c, d, 3, h)
                if h == d:
                    value = value + got_sum(c, d, 4, h)
                send_sum(c, d, 2, h, value)
    grad_slabs(0)

    for c in range(2):
        for h in range(2):
            value = own_part(c, 0, h)
            for k in (1, 2):
                for d in range(2):
                    value = value + got_sum(c, d, k, h)
            two_out[c, half(h)] = value.astype(BF16)
        for o in reversed(OFFS):
            j = zs[o] if c == 0 else ys[o]
            to = at(y, j, 0) if c == 0 else at(j, z, 1)
            send_two = remote(two_out.at[c, j], two_in.at[xl, z if c == 0 else y], s_two, r_two, to)
            if o != 0:
                send_two.start()
            else:
                pl.when(xl != c)(send_two.start)

    @pl.when(has_down)
    def _():
        send_c.wait_recv()
        decoder_grad(1, cprev)

    @pl.when(jnp.logical_not(has_down))
    def _():
        dg_ref[1] = jnp.zeros((64, 4096), BF16)

    out_1 = pltpu.make_async_copy(dg_ref.at[1], dg_hbm.at[1], out_sem.at[1])
    out_1.start()
    arrived(cprev.at[0, pl.ds(0, 5), pl.ds(0, 3)], r_two)
    mine = two_out[xl, line[0][0]].astype(F32) + two_in[1 - xl, line[0][0]].astype(F32)
    for o in OFFS[1:]:
        for p in range(2):
            mine = mine + two_in[p, line[0][o]].astype(F32)

    send_g.wait_recv()
    pre_grad = (mine * 2.0 * active[...]).astype(BF16)

    def enc_step(i, carry):
        block = dot_nt(pre_grad, input_rows(i))
        cols = pl.ds(pl.multiple_of(i * 1024, 1024), 1024)
        eg_ref[:, cols] = block.astype(BF16)
        pltpu.make_async_copy(eg_ref.at[:, cols], eg_hbm.at[:, cols], out_sem.at[2]).start()
        return carry

    lax.fori_loop(0, NY, enc_step, 0, unroll=True)

    pltpu.make_async_copy(eg_ref, eg_hbm, out_sem.at[2]).wait()
    out_0.wait()
    out_1.wait()
    arrived(cod.at[:, 0, pl.ds(0, 7)], s_line.at[0])
    arrived(cod.at[0, pl.ds(0, 5), pl.ds(0, 3)], s_line.at[1])
    for g in range(2):
        arrived(cod.at[:, pl.ds(0, 7)], s_ring.at[g])
    for copy in (send_p, send_s, send_g):
        copy.wait_send()
    arrived(ring_out.at[:, :, :, pl.ds(0, 7)], s_red)
    arrived(cprev.at[0, pl.ds(0, 5), pl.ds(0, 3)], s_two)

    @pl.when(has_down)
    def _():
        send_w.wait_send()
        send_e.wait_send()

    @pl.when(has_up)
    def _():
        send_r.wait_send()
        send_c.wait_send()


def on_device(inputs, targets, enc_w, enc_b, dec_w, dec_b):
    scale = inputs.shape[1] ** (-0.5)
    vmem = pl.BlockSpec(memory_space=pltpu.VMEM)
    hbm = pl.BlockSpec(memory_space=pltpu.HBM)
    dma = pltpu.SemaphoreType.DMA
    grid = (NX, 8, 8, 32, 128)
    eg, dg = pl.pallas_call(
        functools.partial(kernel, scale),
        out_shape=(
            jax.ShapeDtypeStruct((32, 8192), BF16),
            jax.ShapeDtypeStruct((2, 64, 4096), BF16),
        ),
        in_specs=[hbm] * 6,
        out_specs=(hbm, hbm),
        scratch_shapes=[
            pltpu.VMEM((32, 8192), BF16),
            pltpu.VMEM((2, 64, 4096), BF16),
            dma((3,)),
            pltpu.VMEM((NX, NX, 8, 8, 32, 128), BF16),
            pltpu.VMEM(grid, BF16),
            pltpu.VMEM(grid, BF16),
            pltpu.VMEM((32, 128), BF16),
            pltpu.VMEM((64, 128), BF16),
            pltpu.VMEM((1, 32), F32),
            pltpu.VMEM((1, 64), F32),
            pltpu.VMEM((32, 8192), BF16),
            pltpu.VMEM((2, 64, 4096), BF16),
            pltpu.VMEM((64, 4096), BF16),
            pltpu.VMEM((128, 128), BF16),
            pltpu.VMEM((64, 128), F32),
            pltpu.VMEM((128, 128), F32),
            pltpu.VMEM((NX, NX, 8, 32, 256), BF16),
            pltpu.VMEM((NX, 8, 32, 256), BF16),
            pltpu.VMEM((64, 128), F32),
            pltpu.VMEM((32, 128), F32),
            pltpu.VMEM(grid, BF16),
            pltpu.VMEM((NX, 8, 128, 256), BF16),
            pltpu.VMEM((32, 128), F32),
            pltpu.VMEM(grid, F32),
            pltpu.VMEM((2, 2, 4, 8, 32, 128), BF16),
            pltpu.VMEM((2, 2, 4, 8, 32, 128), BF16),
            pltpu.VMEM((2, 8, 32, 128), BF16),
            pltpu.VMEM((2, 8, 32, 128), BF16),
            dma((5,)),
            dma((2,)),
            dma((2, 2)),
            dma((2,)),
            dma((2, 2, 2, 5)),
            dma((7,)),
            dma((7,)),
            dma,
            dma((2, 2, 5)),
            dma,
            dma,
        ],
        compiler_params=pltpu.CompilerParams(collective_id=0, has_side_effects=True),
    )(inputs[0].T, targets[0].T, enc_w[0], enc_b, dec_w[0], dec_b)
    return eg[None], dg[None]


def solution(mesh):
    return jax.shard_map(
        on_device,
        mesh=mesh,
        in_specs=(
            P("section", None, "feat"),
            P("section", None, "feat"),
            P("section", "feat", None),
            P("section", "feat"),
            P("section", None, "feat", None),
            P("section", "feat"),
        ),
        out_specs=(P("section", "feat", None), P("section", None, "feat", None)),
        check_vma=False,
    )
```

```python
import functools

import jax
import jax.numpy as jnp
from jax import lax
from jax.experimental import pallas as pl
from jax.experimental.pallas import tpu as pltpu
from jax.sharding import PartitionSpec as P

MESH = pl.DeviceIdType.MESH
NY, NZ, NX = 8, 8, 2
BF16, F32 = jnp.bfloat16, jnp.float32


def mod(a, n):
    return lax.rem(a + n, n)


def dot(a, b):
    return jnp.dot(a, b, preferred_element_type=F32)


def dot_nt(a, b):
    return lax.dot_general(a, b, (((1,), (1,)), ((), ())), preferred_element_type=F32)


def column(row):
    n = row.shape[1]
    here = lax.broadcasted_iota(jnp.int32, (n, n), 0) == lax.broadcasted_iota(jnp.int32, (n, n), 1)
    return jnp.sum(jnp.where(here, jnp.broadcast_to(row, (n, n)), 0.0), axis=1, keepdims=True)


GROUPS = ((0, 1, -1), (2, -2), (3, -3, 4))
OFFS = tuple(o for group in GROUPS for o in group)


def group_of(o):
    return next(n for n, group in enumerate(GROUPS) if o in group)


def back(o):
    return o if o == 4 else -o


def reach(d, o):
    return 4 if OFFS.index(o) % 2 == d else 3


def travellers(n, d, k):
    return [o for o in GROUPS[n] if k <= reach(d, o)]


PIECES = (2, 2)
LEVELS = (2, 1, 3, 4)


def sem_of(k, h, split):
    return h if k == split else 2 + [n for n in (1, 2, 3, 4) if n != split].index(k)


def carries(g, k, h, d):
    return k < 4 or (d == 0 if PIECES[g] == 1 else h // (PIECES[g] // 2) == d)


def kernel(
    scale, in_hbm, tgt_hbm, encw_hbm, encb_hbm, decw_hbm, decb_hbm,
    eg_hbm, dg_hbm,
    eg_ref, dg_ref, out_sem, gin, cod, cprev, cown, tgt, encb_ref, decb_ref, encw, decw, dwn, err, rprev, sums, encp, encr, pre_sum, pre_in, wt, wp, active, part, ring_in, ring_out, two_in, two_out,
    load_sem, s_line, r_one, s_ring, r_ring, s_sec, r_sec, s_red, r_red, s_two, r_two,
):
    s = lax.axis_index("section")
    f = lax.axis_index("feat")
    xl = lax.rem(f, NX)
    z = lax.rem(f // NX, NZ)
    y = f // (NX * NZ)
    ys = {o: mod(y + o, NY) for o in range(-4, 5)}
    zs = {o: mod(z + o, NZ) for o in range(-4, 5)}

    def at(yy, zz, xx):
        return {"section": s, "feat": (yy * NZ + zz) * NX + xx}

    far_f = (y * NZ + z) * NX + 1 - xl
    odd = lax.rem(s, 2)
    up = {"section": jnp.minimum(s + 1, 3), "feat": jnp.where(odd == 1, far_f, f)}
    down = {"section": jnp.maximum(s - 1, 0), "feat": jnp.where(odd == 0, far_f, f)}
    has_up = s < 3
    has_down = s > 0

    even = xl == 0
    ring = [{o: jnp.where(even, ys[o], zs[o]) for o in ys}, {o: jnp.where(even, zs[o], ys[o]) for o in ys}]
    line = ring[::-1]
    colour = [xl, 1 - xl]

    def along_ring(role, o, xx):
        if role == 0:
            return at(jnp.where(even, ys[o], y), jnp.where(even, z, zs[o]), xx)
        return at(jnp.where(even, y, ys[o]), jnp.where(even, zs[o], z), xx)

    mate = at(y, z, 1 - xl)
    barrier = pltpu.get_barrier_semaphore()
    for o in OFFS:
        if o != 0:
            pl.semaphore_signal(barrier, inc=1, device_id=at(ys[o], z, xl), device_id_type=MESH)
            pl.semaphore_signal(barrier, inc=1, device_id=at(y, zs[o], xl), device_id_type=MESH)
        pl.semaphore_signal(barrier, inc=1, device_id=along_ring(1, o, 1 - xl), device_id_type=MESH)
        if o != 0:
            pl.semaphore_signal(barrier, inc=1, device_id=along_ring(0, o, 1 - xl), device_id_type=MESH)

    @pl.when(has_up)
    def _():
        pl.semaphore_signal(barrier, inc=1, device_id=up, device_id_type=MESH)

    @pl.when(has_down)
    def _():
        pl.semaphore_signal(barrier, inc=1, device_id=down, device_id_type=MESH)

    load_e = pltpu.make_async_copy(encw_hbm, encw, load_sem.at[0])
    load_d = pltpu.make_async_copy(decw_hbm, decw, load_sem.at[1])
    load_t = pltpu.make_async_copy(tgt_hbm, tgt, load_sem.at[2])
    load_b = pltpu.make_async_copy(encb_hbm, encb_ref, load_sem.at[3])
    load_c = pltpu.make_async_copy(decb_hbm, decb_ref, load_sem.at[4])
    for load in (load_d, load_e, load_t, load_b, load_c):
        load.start()

    pl.semaphore_wait(barrier, 29 + jnp.where(has_up, 1, 0) + jnp.where(has_down, 1, 0))

    def remote(src, dst, ss, rs, to):
        return pltpu.make_async_remote_copy(
            src_ref=src, dst_ref=dst, send_sem=ss, recv_sem=rs, device_id=to, device_id_type=MESH
        )

    def arrived(blocks, sem):
        pltpu.make_async_copy(blocks, blocks, sem).wait()

    def place(buf, g, role, i, o):
        if g == 0:
            return buf.at[role, (ys, zs)[role][i], (zs, ys)[role][o]]
        return buf.at[colour[role], ring[role][i], line[role][o]]

    def along(g, role, o, xx):
        if g == 1:
            return along_ring(role, o, xx)
        return at(ys[o], z, xx) if role == 0 else at(y, zs[o], xx)

    def gather(buf, g, sources):
        for role, src in enumerate(sources):
            own = place(buf, g, role, 0, 0)
            pltpu.make_async_copy(src, own, r_one.at[g, role]).start()
            for o in reversed(OFFS):
                if g == 1:
                    remote(src, own, s_line.at[g], r_one.at[g, 1], along(g, 1, o, 1 - xl)).start()
                if o != 0:
                    remote(src, own, s_line.at[g], r_one.at[g, role], along(g, 1 - role, o, xl)).start()

    def gather_rest(buf, g, meanwhile):
        meanwhile(-1)
        blocks = 8 // PIECES[g]

        def piece(role, i, h):
            c, at_ring = (role, (ys, zs)[role]) if g == 0 else (colour[role], ring[role])
            return buf.at[c, at_ring[i], pl.ds(h * blocks, blocks)]

        def send(role, d, k, h):
            way = 1 if d == 0 else -1
            ref = piece(role, 0 if k < 3 else -2 * way, h)
            to = along(g, role, way if k in (1, 3) else 2 * way, xl)
            remote(ref, ref, s_ring.at[g], r_ring.at[g, role, d, sem_of(k, h, 2)], to).start()

        for role in range(2):
            arrived(buf.at[0, 0], r_one.at[g, role])
            for k in (2, 1):
                for h in range(PIECES[g]):
                    for d in range(2):
                        send(role, d, k, h)
        meanwhile(0)
        for k in LEVELS:
            for h in range(PIECES[g]):
                for role in range(2):
                    for d in range(2):
                        i = -k if d == 0 else k
                        if k in (2, 4) and carries(g, k, h, d):
                            arrived(piece(role, i, h), r_ring.at[g, role, d, sem_of(k, h, 2)])
                        elif k in (1, 3) and h == 0:
                            arrived(buf.at[0, 0], r_ring.at[g, role, d, sem_of(k, h, 2)])
                        if k == 2:
                            for further in (4, 3):
                                if carries(g, further, h, d):
                                    send(role, d, further, h)
            meanwhile(k)

    def rows_of(buf, i):
        return jnp.stack([buf[0, i], buf[1, :, i]], axis=1).reshape(-1, 128)

    def input_rows(i):
        parts = [gin[c, 0, i] if r == 0 else gin[c, 1, :, i] for c in range(2) for r in range(2)]
        return jnp.stack(parts, axis=1).reshape(-1, 128)

    send_w = remote(decw.at[1], dwn, s_sec.at[0], r_sec.at[0], down)

    def at_distance(k):
        return (k,) if k in (0, 4) else (k, -k)

    def sort_encoder(i, carry):
        for c in range(2):
            for r in range(2):
                for j in range(2):
                    parts = []
                    for o in range(4 * j, 4 * j + 4):
                        base = i * 1024 + o * 128 if r == 0 else o * 1024 + i * 128
                        first = c * 64 + r * 32
                        parts.append(encw[:, pl.ds(pl.multiple_of(base, 128), 128)][:, first : first + 32])
                    encp[c, r, i, :, j * 128 : j * 128 + 128] = jnp.concatenate(parts, axis=1)
        return carry

    def turn_decoders(i, carry):
        for q in range(4):
            cols = pl.ds(pl.multiple_of(i * 512 + q * 128, 128), 128)
            tile = jnp.concatenate([decw[0, :, cols], dwn[:, cols]], axis=0).T
            for o in range(2):
                wt[0, i, 2 * q + o] = tile[o * 64 : o * 64 + 32]
                wt[1, 2 * q + o, i] = tile[o * 64 + 32 : o * 64 + 64]
        return carry

    send_p = remote(encp.at[1 - xl], encr, s_sec.at[4], r_sec.at[4], mate)
    send_s = remote(pre_sum.at[pl.ds(32, 32)], pre_in, s_sec.at[5], r_sec.at[5], mate)
    send_g = remote(gin.at[xl], gin.at[xl], s_sec.at[6], r_sec.at[6], mate)

    def during_inputs(k):
        if k == -1:
            load_d.wait()
            pl.when(has_down)(send_w.start)
            sums[...] = jnp.zeros_like(sums)
            pre_sum[...] = jnp.zeros_like(pre_sum)
            for load in (load_e, load_t, load_b, load_c):
                load.wait()
            lax.fori_loop(0, 8, sort_encoder, 0)
            send_p.start()
        elif k > 0:
            if k == LEVELS[0]:
                send_p.wait_recv()
            acc = pre_sum[...]
            for i in at_distance(k) + (at_distance(0) if k == LEVELS[0] else ()):
                for role in range(2):
                    r = (ys, zs)[role][i]
                    both = jnp.concatenate([encp[xl, role, r], encr[role, r]], axis=0)
                    acc = acc + dot(both, gin[xl, role, r].reshape(256, 128))
            pre_sum[...] = acc
        if k == LEVELS[0]:
            pl.when(has_up)(send_w.wait_recv)

            @pl.when(jnp.logical_not(has_up))
            def _():
                dwn[...] = jnp.zeros_like(dwn)
                err[pl.ds(64, 64), :] = jnp.zeros((64, 128), BF16)

        if k in LEVELS[:3]:
            turn = 3 * LEVELS.index(k)
            lax.fori_loop(turn, min(turn + 3, 8), turn_decoders, 0)

    def sort_decoders(i, carry):
        for c in range(2):
            wp[c, i] = wt[c, i].reshape(256, 128).T
        return carry

    def during_codes(k):
        if k == -1:
            lax.fori_loop(0, 8, sort_decoders, 0)
        elif k >= 0:
            if k == 0:
                send_g.start()
            acc = sums[...]
            for i in at_distance(k):
                for role in range(2):
                    c, r = colour[role], ring[role][i]
                    acc = acc + dot(wp[c, r], cod[c, r].reshape(256, 128))
            sums[...] = acc

    gather(gin.at[xl], 0, (in_hbm.at[pl.ds(0, 32)], in_hbm.at[pl.ds(32, 32)]))
    gather_rest(gin.at[xl], 0, during_inputs)

    send_s.start()
    pre = pre_sum[pl.ds(0, 32), :] + column(encb_ref[...])
    send_s.wait_recv()
    pre = pre + pre_in[...]
    act = jnp.maximum(pre, 0.0)
    active[...] = act
    cown[...] = (act * act).astype(BF16)
    gather(cod, 1, (cown,))
    gather_rest(cod, 1, during_codes)

    send_r = remote(sums.at[pl.ds(64, 64)], rprev, s_sec.at[1], r_sec.at[1], up)
    send_c = remote(cod, cprev, s_sec.at[2], r_sec.at[2], up)
    send_e = remote(err.at[pl.ds(0, 64)], err.at[pl.ds(64, 64)], s_sec.at[3], r_sec.at[3], down)

    @pl.when(has_up)
    def _():
        send_r.start()
        send_c.start()

    @pl.when(jnp.logical_not(has_down))
    def _():
        rprev[...] = jnp.zeros_like(rprev)

    total = sums[pl.ds(0, 64), :] + column(decb_ref[...])

    @pl.when(has_down)
    def _():
        send_r.wait_recv()

    total = total + rprev[...]
    err[pl.ds(0, 64), :] = ((total - tgt[...].astype(F32)) * scale).astype(BF16)

    @pl.when(has_down)
    def _():
        send_e.start()

    def decoder_grad(slot, codes):
        def step(i, carry):
            block = dot_nt(err[pl.ds(0, 64), :], rows_of(codes, i))
            dg_ref[slot, :, pl.ds(pl.multiple_of(i * 512, 512), 512)] = block.astype(BF16)
            return carry

        lax.fori_loop(0, NY, step, 0)


    @pl.when(has_up)
    def _():
        send_e.wait_recv()

    def grad_slabs(m):
        for i in at_distance(m):
            for c, r in ((0, ys[i]), (1, zs[i])):
                part[c, r] = dot(wt[c, r].reshape(256, 128), err[...]).reshape(8, 32, 128)

    def half(h):
        return pl.ds(4 * h, 4)

    def own_part(c, i, h):
        return part[c, ys[i] if c == 0 else zs[i], half(h)]

    def send_sum(c, d, k, h, value):
        way = 1 if d == 0 else -1
        step = way if k in (1, 3) else 2 * way
        to = at(ys[step], z, xl) if c == 0 else at(y, zs[step], xl)
        ring_out[c, d, k - 1, half(h)] = value.astype(BF16)
        remote(
            ring_out.at[c, d, k - 1, half(h)], ring_in.at[c, d, k - 1, half(h)], s_red, r_red.at[c, d, sem_of(k, h, 3)], to
        ).start()

    def got_sum(c, d, k, h):
        if k > 2:
            arrived(ring_in.at[c, d, k - 1, half(h)], r_red.at[c, d, sem_of(k, h, 3)])
        elif h == 0:
            arrived(ring_in.at[c, d, k - 1], r_red.at[c, d, sem_of(k, h, 3)])
        return ring_in[c, d, k - 1, half(h)].astype(F32)

    for k in (4, 3, 1):
        grad_slabs(k)
        for c in range(2):
            for h in range(2):
                for d in range(2):
                    if k < 4 or h == d:
                        send_sum(c, d, k, h, own_part(c, k if d == 0 else -k, h))
    grad_slabs(2)
    decoder_grad(0, cod)
    out_0 = pltpu.make_async_copy(dg_ref.at[0], dg_hbm.at[0], out_sem.at[0])
    out_0.start()
    for h in range(2):
        for c in range(2):
            for d in range(2):
                value = own_part(c, 2 if d == 0 else -2, h) + got_sum(c, d, 3, h)
                if h == d:
                    value = value + got_sum(c, d, 4, h)
                send_sum(c, d, 2, h, value)
    grad_slabs(0)

    for c in range(2):
        for h in range(2):
            value = own_part(c, 0, h)
            for k in (1, 2):
                for d in range(2):
                    value = value + got_sum(c, d, k, h)
            two_out[c, half(h)] = value.astype(BF16)
        for o in reversed(OFFS):
            j = zs[o] if c == 0 else ys[o]
            to = at(y, j, 0) if c == 0 else at(j, z, 1)
            send_two = remote(two_out.at[c, j], two_in.at[xl, z if c == 0 else y], s_two, r_two, to)
            if o != 0:
                send_two.start()
            else:
                pl.when(xl != c)(send_two.start)

    @pl.when(has_down)
    def _():
        send_c.wait_recv()
        decoder_grad(1, cprev)

    @pl.when(jnp.logical_not(has_down))
    def _():
        dg_ref[1] = jnp.zeros((64, 4096), BF16)

    out_1 = pltpu.make_async_copy(dg_ref.at[1], dg_hbm.at[1], out_sem.at[1])
    out_1.start()
    arrived(cprev.at[0, pl.ds(0, 5), pl.ds(0, 3)], r_two)
    mine = two_out[xl, line[0][0]].astype(F32) + two_in[1 - xl, line[0][0]].astype(F32)
    for o in OFFS[1:]:
        for p in range(2):
            mine = mine + two_in[p, line[0][o]].astype(F32)

    send_g.wait_recv()
    pre_grad = (mine * 2.0 * active[...]).astype(BF16)

    def enc_step(i, carry):
        block = dot_nt(pre_grad, input_rows(i))
        cols = pl.ds(pl.multiple_of(i * 1024, 1024), 1024)
        eg_ref[:, cols] = block.astype(BF16)
        pltpu.make_async_copy(eg_ref.at[:, cols], eg_hbm.at[:, cols], out_sem.at[2]).start()
        return carry

    lax.fori_loop(0, NY, enc_step, 0, unroll=True)

    pltpu.make_async_copy(eg_ref, eg_hbm, out_sem.at[2]).wait()
    out_0.wait()
    out_1.wait()
    arrived(cod.at[:, 0, pl.ds(0, 7)], s_line.at[0])
    arrived(cod.at[0, pl.ds(0, 5), pl.ds(0, 3)], s_line.at[1])
    for g in range(2):
        arrived(cod.at[:, pl.ds(0, 7)], s_ring.at[g])
    for copy in (send_p, send_s, send_g):
        copy.wait_send()
    arrived(ring_out.at[:, :, :, pl.ds(0, 7)], s_red)
    arrived(cprev.at[0, pl.ds(0, 5), pl.ds(0, 3)], s_two)

    @pl.when(has_down)
    def _():
        send_w.wait_send()
        send_e.wait_send()

    @pl.when(has_up)
    def _():
        send_r.wait_send()
        send_c.wait_send()


def on_device(inputs, targets, enc_w, enc_b, dec_w, dec_b):
    scale = inputs.shape[1] ** (-0.5)
    vmem = pl.BlockSpec(memory_space=pltpu.VMEM)
    hbm = pl.BlockSpec(memory_space=pltpu.HBM)
    dma = pltpu.SemaphoreType.DMA
    grid = (NX, 8, 8, 32, 128)
    eg, dg = pl.pallas_call(
        functools.partial(kernel, scale),
        out_shape=(
            jax.ShapeDtypeStruct((32, 8192), BF16),
            jax.ShapeDtypeStruct((2, 64, 4096), BF16),
        ),
        in_specs=[hbm] * 6,
        out_specs=(hbm, hbm),
        scratch_shapes=[
            pltpu.VMEM((32, 8192), BF16),
            pltpu.VMEM((2, 64, 4096), BF16),
            dma((3,)),
            pltpu.VMEM((NX, NX, 8, 8, 32, 128), BF16),
            pltpu.VMEM(grid, BF16),
            pltpu.VMEM(grid, BF16),
            pltpu.VMEM((32, 128), BF16),
            pltpu.VMEM((64, 128), BF16),
            pltpu.VMEM((1, 32), F32),
            pltpu.VMEM((1, 64), F32),
            pltpu.VMEM((32, 8192), BF16),
            pltpu.VMEM((2, 64, 4096), BF16),
            pltpu.VMEM((64, 4096), BF16),
            pltpu.VMEM((128, 128), BF16),
            pltpu.VMEM((64, 128), F32),
            pltpu.VMEM((128, 128), F32),
            pltpu.VMEM((NX, NX, 8, 32, 256), BF16),
            pltpu.VMEM((NX, 8, 32, 256), BF16),
            pltpu.VMEM((64, 128), F32),
            pltpu.VMEM((32, 128), F32),
            pltpu.VMEM(grid, BF16),
            pltpu.VMEM((NX, 8, 128, 256), BF16),
            pltpu.VMEM((32, 128), F32),
            pltpu.VMEM(grid, F32),
            pltpu.VMEM((2, 2, 4, 8, 32, 128), BF16),
            pltpu.VMEM((2, 2, 4, 8, 32, 128), BF16),
            pltpu.VMEM((2, 8, 32, 128), BF16),
            pltpu.VMEM((2, 8, 32, 128), BF16),
            dma((5,)),
            dma((2,)),
            dma((2, 2)),
            dma((2,)),
            dma((2, 2, 2, 5)),
            dma((7,)),
            dma((7,)),
            dma,
            dma((2, 2, 5)),
            dma,
            dma,
        ],
        compiler_params=pltpu.CompilerParams(collective_id=0, has_side_effects=True),
    )(inputs[0].T, targets[0].T, enc_w[0], enc_b, dec_w[0], dec_b)
    return eg[None], dg[None]


def solution(mesh):
    return jax.shard_map(
        on_device,
        mesh=mesh,
        in_specs=(
            P("section", None, "feat"),
            P("section", None, "feat"),
            P("section", "feat", None),
            P("section", "feat"),
            P("section", None, "feat", None),
            P("section", "feat"),
        ),
        out_specs=(P("section", "feat", None), P("section", None, "feat", None)),
        check_vma=False,
    )
```
